512 devices in a mesh: sta: 64 (over y, z_hi, x), stk: 8 (over z_lo, core).
Axes of the slice: x: 4, y: 8, z: 8 (z_hi: 2, z_lo: 4; z = z_hi * 4 + z_lo), core: 2. Of those that a mesh axis runs over, the one named last changes fastest.
Arguments:
- spectra: float32 [8, 256, 2, 2048], P('stk', 'sta')
- partner_masks: int32 [4], replicated, may hold values from 1 to 63, as said below
Outputs:
- correlations: float32 [1024, 4, 2400], P(('sta', 'stk'))
The draws below stay inside these ranges and needn't reach their ends.
Inputs may be any that keep to these rules, and one draw needn't show every extreme that they name: `partner_masks`: each round's block pairing is b with b XOR mask; every bit below log2 of the number of station blocks is set in some round's mask.
All inputs are finite; a program needn't handle non-finite values.
Results may differ from the reference program's by a relative error of at most 0.0037.
Values may be sent and summed in bfloat16 or wider, within the bound.
No kernel may reach another device: no remote copies, remote signals or barrier semaphores. Data moves between devices by JAX's collectives and lax.ppermute only.
A program may use at most 64 MiB of HBM per device.

```python
import jax
import jax.numpy as jnp
from jax import lax

SB = 4
ROUNDS = 4
FB = 2048
NFFT = 8192
MAXLAG = 1200
STATIONS = 256
WINDOWS = 8
N_STA = 64


def draw_spectra(key, part):
    first_key, second_key, third_key = jax.random.split(key, 3)
    shape_full = (WINDOWS, STATIONS, 2, FB)
    noise = jax.random.normal(first_key, shape_full, jnp.float32)
    log_bins = jax.random.uniform(second_key, (WINDOWS, STATIONS, 1, FB), jnp.float32, -2.3, 2.3)
    log_station = jax.random.uniform(third_key, (1, STATIONS, 1, 1), jnp.float32, -1.15, 1.15)
    return noise * jnp.exp(log_bins + log_station)


def draw_partner_masks(key, part):
    raw_masks = jax.random.randint(key, (ROUNDS,), 1, N_STA, jnp.int32)
    covered = jnp.bitwise_or(raw_masks[0], jnp.bitwise_xor(raw_masks[1], N_STA - 1))
    return raw_masks.at[0].set(covered)


def setup_inputs(seed: int = 0) -> dict:
    key_of = jax.random.split(jax.random.key(seed), 3)
    return {
        "spectra": draw_spectra(jax.random.fold_in(key_of[2], 71), 0),
        "partner_masks": draw_partner_masks(jax.random.fold_in(key_of[2], 71), 0),
    }


def reference(spectra, partner_masks):
    power_spec = spectra[:, :, 0] ** 2 + spectra[:, :, 1] ** 2
    water_base = lax.optimization_barrier(jnp.mean(power_spec, axis=-1, keepdims=True))
    denom = jnp.sqrt(power_spec + 0.05 * (water_base + 1e-06))
    whitened = (spectra / denom[:, :, None, :]).astype(jnp.bfloat16).astype(jnp.float32)
    blocks = whitened.reshape(WINDOWS, N_STA, SB, 2, FB)
    normalizer = 1.0 / jnp.sqrt(jnp.float32(WINDOWS * FB))

    def one_round(round_mask):
        block_ids = jnp.arange(N_STA, dtype=jnp.int32)
        partner_ids = jnp.bitwise_xor(block_ids, round_mask.astype(jnp.int32))
        partner_blocks = jnp.take(blocks, partner_ids, axis=1)
        own_re = blocks[:, :, :, 0]
        own_im = blocks[:, :, :, 1]
        far_re = partner_blocks[:, :, :, 0]
        far_im = partner_blocks[:, :, :, 1]
        real_part = jnp.einsum('wbik,wbjk->bijk', own_re, far_re) + jnp.einsum('wbik,wbjk->bijk', own_im, far_im)
        imag_part = jnp.einsum('wbik,wbjk->bijk', own_im, far_re) - jnp.einsum('wbik,wbjk->bijk', own_re, far_im)
        spectrum = lax.complex(real_part, imag_part)
        padded = jnp.pad(spectrum, ((0, 0), (0, 0), (0, 0), (0, NFFT // 2 + 1 - FB)))
        series = jnp.fft.irfft(padded, n=NFFT, axis=-1) * NFFT * normalizer
        lagged = jnp.concatenate([series[..., NFFT - MAXLAG:], series[..., :MAXLAG]], axis=-1)
        return lagged.reshape(N_STA * SB * SB, 2 * MAXLAG)
    per_round = lax.map(one_round, partner_masks)
    return jnp.transpose(per_round, (1, 0, 2))
```

```python
import functools
import math

import jax
import jax.numpy as jnp
import numpy as np
from jax import lax
from jax.experimental import pallas as pl
from jax.experimental.pallas import tpu as pltpu
from jax.sharding import Mesh, PartitionSpec as P

NFFT = 8192
MAXLAG = 1200
LANES = 128
STATIONS_HERE = 4
ROUNDS = 4
WINDOWS = 8
COARSE = 16
SHARES = 64
PAIR_LANES = 64
GROUPS = 19
GROUP_ROWS = 80
INTERPRET = False

VMEM = pltpu.MemorySpace.VMEM
SMEM = pltpu.MemorySpace.SMEM


def split_bf16(table):
    high = table.astype(jnp.bfloat16)
    low = (table - high.astype(np.float64)).astype(jnp.bfloat16)
    return high, low


@functools.lru_cache(None)
def selection_tables():
    lane = np.arange(LANES)
    coarse, station, part = lane // 8, lane // 2 % 4, lane % 2
    half, out_coarse, low, out_part = lane // 64, lane // 4 % 16, lane // 2 % 2, lane % 2
    same_bin = coarse[:, None] == out_coarse[None, :]
    own = [
        same_bin & (station == i)[:, None] & (part == c)[:, None]
        for c in range(2)
        for i in range(STATIONS_HERE)
    ]
    far_station = same_bin & (station[:, None] == (2 * half + low)[None, :])
    match = (part[:, None] == out_part[None, :]) & far_station
    cross = (part[:, None] != out_part[None, :]) & far_station
    sign = np.where(out_part == 1, -1.0, 1.0)
    return (
        np.concatenate(own, axis=1).astype(jnp.bfloat16),
        np.concatenate([match * sign, cross * 1.0], axis=1).astype(jnp.bfloat16),
    )


@functools.lru_cache(None)
def transform_tables():
    f = np.arange(LANES)
    shift = -MAXLAG % LANES
    base = (MAXLAG + shift) // LANES
    lane = np.arange(PAIR_LANES)
    coarse, pair, part = lane // 4, lane // 2 % 2, lane % 2
    angle = 2 * np.pi * (coarse[:, None] * (f + shift)[None, :] % 64) / 64
    cos, sin = np.cos(angle), np.sin(angle)
    real = np.where(part[:, None] == 0, cos, -sin)
    imag = np.where(part[:, None] == 0, sin, cos)
    first = np.concatenate(
        [
            np.where((pair == p)[:, None], value, 0.0)
            for p in range(2)
            for value in (real, imag)
        ],
        axis=1,
    )
    first = np.concatenate(split_bf16(first), axis=0)
    row = np.arange(SHARES * 8)
    fine = 2 * (row // 8) + row % 2
    twist = 2 * np.pi * (fine[:, None] * (f + shift)[None, :] % NFFT) / NFFT
    out_row = np.arange(GROUP_ROWS)
    group, out_round = out_row // ROUNDS, out_row % ROUNDS
    in_row = np.arange(SHARES // 2 * 8)
    in_fine, in_round = 2 * (in_row // 8) + in_row % 2, in_row // 2 % ROUNDS
    last = 2 * np.pi * (in_fine[None, :] * (group - base)[:, None] % 64) / 64
    keep = (out_round[:, None] == in_round[None, :]) & (group < GROUPS)[:, None]
    scale = 2.0 / math.sqrt(WINDOWS * COARSE * LANES)
    cos_hi, cos_lo = split_bf16(np.where(keep, np.cos(last) * scale, 0.0))
    sin_hi, sin_lo = split_bf16(np.where(keep, -np.sin(last) * scale, 0.0))
    return (
        first,
        np.cos(twist).astype(np.float32),
        np.sin(twist).astype(np.float32),
        np.stack([cos_hi, cos_lo, sin_hi, sin_lo]),
    )


def whiten_kernel(spectra_ref, out_ref, rows_ref):
    for station in range(STATIONS_HERE):
        value = spectra_ref[0, station]
        power = jnp.sum(value * value, axis=0, keepdims=True)
        level = jnp.mean(power, axis=1, keepdims=True)
        denom = jnp.sqrt(power + 0.05 * (level + 1e-06))
        white = value / denom
        for coarse in range(COARSE):
            rows_ref[pl.ds(coarse * 8 + station * 2, 2), :] = white[
                :, coarse * LANES : (coarse + 1) * LANES
            ]
    turned = rows_ref[...].T.astype(jnp.bfloat16)
    for copy in range(out_ref.shape[0]):
        out_ref[copy] = turned


def cross_kernel(mask_ref, home_ref, all_ref, own_table, far_table, out_ref, far_ref, left, right):
    home = home_ref[0]
    own = all_ref[pl.ds(pl.multiple_of(home * 128, 128), 128), :]
    left[...] = jnp.dot(own, own_table[...], preferred_element_type=jnp.float32)
    for r in range(ROUNDS):
        mask = mask_ref[r]
        high = (home ^ (mask >> 3)) & 7
        for block in range(8):
            other = (block ^ mask) & 7
            start = pl.multiple_of(high * 128 + other * 16, 16)
            far_ref[pl.ds(r * 128 + block * 16, 16), :] = all_ref[pl.ds(start, 16), :]
    right[...] = jnp.dot(far_ref[...], far_table[...], preferred_element_type=jnp.float32)
    sublane = lax.broadcasted_iota(jnp.int32, (8, LANES), 0)
    lower = lax.broadcasted_iota(jnp.int32, (8, LANES), 1) < PAIR_LANES

    for block in range(8):
        tiles = []
        for i in range(STATIONS_HERE):
            tile = None
            for r in range(ROUNDS):
                total = None
                for step in range(2):
                    rows = pl.ds(block * 16 + step * 8, 8)
                    far_rows = pl.ds(r * 128 + block * 16 + step * 8, 8)
                    for part in range(2):
                        term = (
                            left[rows, pl.ds((part * 4 + i) * LANES, LANES)]
                            * right[far_rows, pl.ds(part * LANES, LANES)]
                        )
                        total = term if total is None else total + term
                total = total + pltpu.roll(total, 4, 0)
                total = total + pltpu.roll(total, 2, 0)
                tile = total if tile is None else jnp.where(sublane >= 2 * r, total, tile)
            turned = pltpu.roll(tile, PAIR_LANES, 1)
            first = jnp.where(lower, tile, turned)
            second = jnp.where(lower, turned, tile)
            tiles += [first, second]
        for index, tile in enumerate(tiles):
            out_ref[block * 8 + index] = tile.astype(jnp.bfloat16)


def transform_kernel(spec_ref, first_ref, cos_ref, sin_ref, last_ref, out_ref, mid_ref):
    row = lax.broadcasted_iota(jnp.int32, (8, LANES), 0)
    lane = lax.broadcasted_iota(jnp.int32, (8, LANES), 1) % PAIR_LANES
    zero_bin = (row % 2 == 0) & (lane < 4)
    head = spec_ref[pl.ds(0, 8), :].astype(jnp.float32)
    head = jnp.where(zero_bin, 0.5 * head, head).astype(jnp.bfloat16)
    spec = jnp.concatenate([head, spec_ref[pl.ds(8, SHARES * 8 - 8), :]], axis=0)
    mid_ref[...] = jnp.dot(spec, first_ref[...], preferred_element_type=jnp.float32)
    half = SHARES * 4
    real, imag = [], []
    for pair in range(2):
        parts_re, parts_im = [], []
        for side in range(2):
            rows = pl.ds(side * half, half)
            y_re = mid_ref[rows, pl.ds(pair * 256, LANES)]
            y_im = mid_ref[rows, pl.ds(pair * 256 + LANES, LANES)]
            c, s = cos_ref[rows, :], sin_ref[rows, :]
            parts_re.append(y_re * c - y_im * s)
            parts_im.append(y_re * s + y_im * c)
        real.append(parts_re[0] + parts_re[1])
        imag.append(parts_im[0] + parts_im[1])
    total = None
    for index, value in ((0, jnp.concatenate(real, axis=1)), (2, jnp.concatenate(imag, axis=1))):
        high = value.astype(jnp.bfloat16)
        low = (value - high.astype(jnp.float32)).astype(jnp.bfloat16)
        for table, operand in ((index, high), (index + 1, high), (index, low)):
            term = jnp.dot(last_ref[table], operand, preferred_element_type=jnp.float32)
            total = term if total is None else total + term
    lags = out_ref.shape[2]
    for pair in range(2):
        for group in range(GROUPS):
            width = min(LANES, lags - group * LANES)
            out_ref[pair, :, pl.ds(group * LANES, width)] = total[
                group * ROUNDS : (group + 1) * ROUNDS, pair * LANES : pair * LANES + width
            ]


def spec_of(space):
    return pl.BlockSpec(memory_space=space)


def whiten(spectra, copies):
    return pl.pallas_call(
        whiten_kernel,
        out_shape=jax.ShapeDtypeStruct((copies, LANES, LANES), jnp.bfloat16),
        in_specs=[spec_of(VMEM)],
        out_specs=spec_of(VMEM),
        scratch_shapes=[pltpu.VMEM((LANES, LANES), jnp.float32)],
        name="whiten",
        interpret=INTERPRET,
    )(spectra)


def cross(partner_masks, home, gathered):
    own_table, far_table = selection_tables()
    return pl.pallas_call(
        cross_kernel,
        out_shape=jax.ShapeDtypeStruct((SHARES, 8, LANES), jnp.bfloat16),
        in_specs=[spec_of(SMEM)] * 2 + [spec_of(VMEM)] * 3,
        out_specs=spec_of(VMEM),
        scratch_shapes=[
            pltpu.VMEM((512, LANES), jnp.bfloat16),
            pltpu.VMEM((LANES, 1024), jnp.float32),
            pltpu.VMEM((512, 256), jnp.float32),
        ],
        name="cross",
        interpret=INTERPRET,
    )(partner_masks, home, gathered, jnp.asarray(own_table), jnp.asarray(far_table))


def transform(spec_rows):
    tables = [jnp.asarray(table) for table in transform_tables()]
    return pl.pallas_call(
        transform_kernel,
        out_shape=jax.ShapeDtypeStruct((2, ROUNDS, 2 * MAXLAG), jnp.float32),
        in_specs=[spec_of(VMEM)] * 5,
        out_specs=spec_of(VMEM),
        scratch_shapes=[pltpu.VMEM((SHARES * 8, 512), jnp.float32)],
        name="transform",
        interpret=INTERPRET,
    )(spec_rows, *tables)


def body(spectra, partner_masks):
    rows = whiten(spectra, lax.axis_size("high"))
    slots = rows.reshape(512, 2, LANES)
    gathered = lax.all_to_all(slots, ("high", "low", "stk"), 0, 0, tiled=True)
    home = lax.axis_index("high").astype(jnp.int32).reshape(1)
    spec = cross(partner_masks, home, gathered.reshape(1024, LANES))
    owned = lax.all_to_all(spec, ("low", "stk"), 0, 0, tiled=True)
    return transform(owned.reshape(SHARES * 8, LANES))


def solution(mesh):
    devices = mesh.devices
    fine = Mesh(devices.reshape(8, devices.shape[0] // 8, devices.shape[1]), ("high", "low", "stk"))
    return jax.shard_map(
        body,
        mesh=fine,
        in_specs=(P("stk", ("high", "low"), None, None), P()),
        out_specs=P(("high", "low", "stk"), None, None),
        check_vma=False,
    )
```

```python
import functools
import math

import jax
import jax.numpy as jnp
import numpy as np
from jax import lax
from jax.experimental import pallas as pl
from jax.experimental.pallas import tpu as pltpu
from jax.sharding import Mesh, PartitionSpec as P

NFFT = 8192
MAXLAG = 1200
LANES = 128
STATIONS_HERE = 4
ROUNDS = 4
WINDOWS = 8
COARSE = 16
SHARES = 64
PAIR_LANES = 64
GROUPS = 19
GROUP_ROWS = 80
INTERPRET = False

VMEM = pltpu.MemorySpace.VMEM
SMEM = pltpu.MemorySpace.SMEM


def split_bf16(table):
    high = table.astype(jnp.bfloat16)
    low = (table - high.astype(np.float64)).astype(jnp.bfloat16)
    return high, low


@functools.lru_cache(None)
def selection_tables():
    lane = np.arange(LANES)
    coarse, station, part = lane // 8, lane // 2 % 4, lane % 2
    half, out_coarse, low, out_part = lane // 64, lane // 4 % 16, lane // 2 % 2, lane % 2
    same_bin = coarse[:, None] == out_coarse[None, :]
    own = [
        same_bin & (station == i)[:, None] & (part == c)[:, None]
        for c in range(2)
        for i in range(STATIONS_HERE)
    ]
    far_station = same_bin & (station[:, None] == (2 * half + low)[None, :])
    match = (part[:, None] == out_part[None, :]) & far_station
    cross = (part[:, None] != out_part[None, :]) & far_station
    sign = np.where(out_part == 1, -1.0, 1.0)
    return (
        np.concatenate(own, axis=1).astype(jnp.bfloat16),
        np.concatenate([match * sign, cross * 1.0], axis=1).astype(jnp.bfloat16),
    )


@functools.lru_cache(None)
def transform_tables():
    f = np.arange(LANES)
    shift = -MAXLAG % LANES
    base = (MAXLAG + shift) // LANES
    lane = np.arange(PAIR_LANES)
    coarse, pair, part = lane // 4, lane // 2 % 2, lane % 2
    angle = 2 * np.pi * (coarse[:, None] * (f + shift)[None, :] % 64) / 64
    cos, sin = np.cos(angle), np.sin(angle)
    real = np.where(part[:, None] == 0, cos, -sin)
    imag = np.where(part[:, None] == 0, sin, cos)
    first = np.concatenate(
        [
            np.where((pair == p)[:, None], value, 0.0)
            for p in range(2)
            for value in (real, imag)
        ],
        axis=1,
    )
    first = np.concatenate(split_bf16(first), axis=0)
    row = np.arange(SHARES * 8)
    fine = 2 * (row // 8) + row % 2
    twist = 2 * np.pi * (fine[:, None] * (f + shift)[None, :] % NFFT) / NFFT
    out_row = np.arange(GROUP_ROWS)
    group, out_round = out_row // ROUNDS, out_row % ROUNDS
    in_row = np.arange(SHARES // 2 * 8)
    in_fine, in_round = 2 * (in_row // 8) + in_row % 2, in_row // 2 % ROUNDS
    last = 2 * np.pi * (in_fine[None, :] * (group - base)[:, None] % 64) / 64
    keep = (out_round[:, None] == in_round[None, :]) & (group < GROUPS)[:, None]
    scale = 2.0 / math.sqrt(WINDOWS * COARSE * LANES)
    cos_hi, cos_lo = split_bf16(np.where(keep, np.cos(last) * scale, 0.0))
    sin_hi, sin_lo = split_bf16(np.where(keep, -np.sin(last) * scale, 0.0))
    return (
        first,
        np.cos(twist).astype(np.float32),
        np.sin(twist).astype(np.float32),
        np.stack([cos_hi, cos_lo, sin_hi, sin_lo]),
    )


def whiten_kernel(spectra_ref, out_ref, rows_ref):
    for station in range(STATIONS_HERE):
        value = spectra_ref[0, station]
        power = jnp.sum(value * value, axis=0, keepdims=True)
        level = jnp.mean(power, axis=1, keepdims=True)
        denom = jnp.sqrt(power + 0.05 * (level + 1e-06))
        white = value / denom
        for coarse in range(COARSE):
            rows_ref[pl.ds(coarse * 8 + station * 2, 2), :] = white[
                :, coarse * LANES : (coarse + 1) * LANES
            ]
    turned = rows_ref[...].T.astype(jnp.bfloat16)
    for copy in range(out_ref.shape[0]):
        out_ref[copy] = turned


def cross_kernel(mask_ref, home_ref, all_ref, own_table, far_table, out_ref, far_ref, left, right):
    home = home_ref[0]
    own = all_ref[pl.ds(pl.multiple_of(home * 128, 128), 128), :]
    left[...] = jnp.dot(own, own_table[...], preferred_element_type=jnp.float32)
    for r in range(ROUNDS):
        mask = mask_ref[r]
        high = (home ^ (mask >> 3)) & 7
        for block in range(8):
            other = (block ^ mask) & 7
            start = pl.multiple_of(high * 128 + other * 16, 16)
            far_ref[pl.ds(r * 128 + block * 16, 16), :] = all_ref[pl.ds(start, 16), :]
    right[...] = jnp.dot(far_ref[...], far_table[...], preferred_element_type=jnp.float32)
    sublane = lax.broadcasted_iota(jnp.int32, (8, LANES), 0)
    lower = lax.broadcasted_iota(jnp.int32, (8, LANES), 1) < PAIR_LANES

    for block in range(8):
        tiles = []
        for i in range(STATIONS_HERE):
            tile = None
            for r in range(ROUNDS):
                total = None
                for step in range(2):
                    rows = pl.ds(block * 16 + step * 8, 8)
                    far_rows = pl.ds(r * 128 + block * 16 + step * 8, 8)
                    for part in range(2):
                        term = (
                            left[rows, pl.ds((part * 4 + i) * LANES, LANES)]
                            * right[far_rows, pl.ds(part * LANES, LANES)]
                        )
                        total = term if total is None else total + term
                total = total + pltpu.roll(total, 4, 0)
                total = total + pltpu.roll(total, 2, 0)
                tile = total if tile is None else jnp.where(sublane >= 2 * r, total, tile)
            turned = pltpu.roll(tile, PAIR_LANES, 1)
            first = jnp.where(lower, tile, turned)
            second = jnp.where(lower, turned, tile)
            tiles += [first, second]
        for index, tile in enumerate(tiles):
            out_ref[block * 8 + index] = tile.astype(jnp.bfloat16)


def transform_kernel(spec_ref, first_ref, cos_ref, sin_ref, last_ref, out_ref, mid_ref):
    row = lax.broadcasted_iota(jnp.int32, (8, LANES), 0)
    lane = lax.broadcasted_iota(jnp.int32, (8, LANES), 1) % PAIR_LANES
    zero_bin = (row % 2 == 0) & (lane < 4)
    head = spec_ref[pl.ds(0, 8), :].astype(jnp.float32)
    head = jnp.where(zero_bin, 0.5 * head, head).astype(jnp.bfloat16)
    spec = jnp.concatenate([head, spec_ref[pl.ds(8, SHARES * 8 - 8), :]], axis=0)
    mid_ref[...] = jnp.dot(spec, first_ref[...], preferred_element_type=jnp.float32)
    half = SHARES * 4
    real, imag = [], []
    for pair in range(2):
        parts_re, parts_im = [], []
        for side in range(2):
            rows = pl.ds(side * half, half)
            y_re = mid_ref[rows, pl.ds(pair * 256, LANES)]
            y_im = mid_ref[rows, pl.ds(pair * 256 + LANES, LANES)]
            c, s = cos_ref[rows, :], sin_ref[rows, :]
            parts_re.append(y_re * c - y_im * s)
            parts_im.append(y_re * s + y_im * c)
        real.append(parts_re[0] + parts_re[1])
        imag.append(parts_im[0] + parts_im[1])
    total = None
    for index, value in ((0, jnp.concatenate(real, axis=1)), (2, jnp.concatenate(imag, axis=1))):
        high = value.astype(jnp.bfloat16)
        low = (value - high.astype(jnp.float32)).astype(jnp.bfloat16)
        for table, operand in ((index, high), (index + 1, high), (index, low)):
            term = jnp.dot(last_ref[table], operand, preferred_element_type=jnp.float32)
            total = term if total is None else total + term
    lags = out_ref.shape[2]
    for pair in range(2):
        for group in range(GROUPS):
            width = min(LANES, lags - group * LANES)
            out_ref[pair, :, pl.ds(group * LANES, width)] = total[
                group * ROUNDS : (group + 1) * ROUNDS, pair * LANES : pair * LANES + width
            ]


def spec_of(space):
    return pl.BlockSpec(memory_space=space)


def in_vmem(array):
    return pltpu.with_memory_space_constraint(jnp.asarray(array), VMEM)


def whiten(spectra, copies):
    return pl.pallas_call(
        whiten_kernel,
        out_shape=pltpu.VMEM((copies, LANES, LANES), jnp.bfloat16),
        in_specs=[spec_of(VMEM)],
        out_specs=spec_of(VMEM),
        scratch_shapes=[pltpu.VMEM((LANES, LANES), jnp.float32)],
        name="whiten",
        interpret=INTERPRET,
    )(spectra)


def cross(partner_masks, home, gathered):
    own_table, far_table = selection_tables()
    return pl.pallas_call(
        cross_kernel,
        out_shape=pltpu.VMEM((SHARES, 8, LANES), jnp.bfloat16),
        in_specs=[spec_of(SMEM)] * 2 + [spec_of(VMEM)] * 3,
        out_specs=spec_of(VMEM),
        scratch_shapes=[
            pltpu.VMEM((512, LANES), jnp.bfloat16),
            pltpu.VMEM((LANES, 1024), jnp.float32),
            pltpu.VMEM((512, 256), jnp.float32),
        ],
        name="cross",
        interpret=INTERPRET,
    )(partner_masks, home, *map(in_vmem, (gathered, own_table, far_table)))


def transform(spec_rows):
    return pl.pallas_call(
        transform_kernel,
        out_shape=jax.ShapeDtypeStruct((2, ROUNDS, 2 * MAXLAG), jnp.float32),
        in_specs=[spec_of(VMEM)] * 5,
        out_specs=spec_of(VMEM),
        scratch_shapes=[pltpu.VMEM((SHARES * 8, 512), jnp.float32)],
        name="transform",
        interpret=INTERPRET,
    )(*map(in_vmem, (spec_rows, *transform_tables())))


def body(spectra, partner_masks):
    rows = whiten(spectra, lax.axis_size("high"))
    slots = rows.reshape(512, 2, LANES)
    gathered = lax.all_to_all(slots, ("high", "low", "stk"), 0, 0, tiled=True)
    home = lax.axis_index("high").astype(jnp.int32).reshape(1)
    spec = cross(partner_masks, home, gathered.reshape(1024, LANES))
    owned = lax.all_to_all(spec, ("low", "stk"), 0, 0, tiled=True)
    return transform(owned.reshape(SHARES * 8, LANES))


def solution(mesh):
    devices = mesh.devices
    fine = Mesh(devices.reshape(8, devices.shape[0] // 8, devices.shape[1]), ("high", "low", "stk"))
    return jax.shard_map(
        body,
        mesh=fine,
        in_specs=(P("stk", ("high", "low"), None, None), P()),
        out_specs=P(("high", "low", "stk"), None, None),
        check_vma=False,
    )
```

```python
import functools
import math

import jax
import jax.numpy as jnp
import numpy as np
from jax import lax
from jax.experimental import pallas as pl
from jax.experimental.pallas import tpu as pltpu
from jax.sharding import Mesh, PartitionSpec as P

NFFT = 8192
MAXLAG = 1200
LANES = 128
STATIONS_HERE = 4
ROUNDS = 4
WINDOWS = 8
COARSE = 16
SHARES = 32
SLOTS = 64
PAIR_LANES = 64
GROUPS = 19
GROUP_ROWS = 80
INTERPRET = False

VMEM = pltpu.MemorySpace.VMEM
SMEM = pltpu.MemorySpace.SMEM


def split_bf16(table):
    high = table.astype(jnp.bfloat16)
    low = (table - high.astype(np.float64)).astype(jnp.bfloat16)
    return high, low


@functools.lru_cache(None)
def selection_tables():
    lane = np.arange(LANES)
    coarse, station, part = lane // 8, lane // 2 % 4, lane % 2
    half, out_coarse, low, out_part = lane // 64, lane // 4 % 16, lane // 2 % 2, lane % 2
    same_bin = coarse[:, None] == out_coarse[None, :]
    own = [
        same_bin & (station == i)[:, None] & (part == c)[:, None]
        for c in range(2)
        for i in range(STATIONS_HERE)
    ]
    far_station = same_bin & (station[:, None] == (2 * half + low)[None, :])
    match = (part[:, None] == out_part[None, :]) & far_station
    cross = (part[:, None] != out_part[None, :]) & far_station
    sign = np.where(out_part == 1, -1.0, 1.0)
    return (
        np.concatenate(own, axis=1).astype(jnp.bfloat16),
        np.concatenate([match * sign, cross * 1.0], axis=1).astype(jnp.bfloat16),
    )


@functools.lru_cache(None)
def transform_tables():
    f = np.arange(LANES)
    shift = -MAXLAG % LANES
    base = (MAXLAG + shift) // LANES
    lane = np.arange(LANES)
    in_bit, coarse, pair, part = lane // 64, lane // 4 % 16, lane // 2 % 2, lane % 2
    angle = 2 * np.pi * (coarse[:, None] * (f + shift)[None, :] % 64) / 64
    cos, sin = np.cos(angle), np.sin(angle)
    real = np.where(part[:, None] == 0, cos, -sin)
    imag = np.where(part[:, None] == 0, sin, cos)
    first = np.concatenate(
        [
            np.where(((pair == p) & (in_bit == bit))[:, None], value, 0.0)
            for bit in range(2)
            for p in range(2)
            for value in (real, imag)
        ],
        axis=1,
    )
    first_hi, first_lo = split_bf16(first)
    first = np.concatenate([first_hi, first_hi, first_lo], axis=0)
    row = np.arange(SHARES * 8)
    fine = 4 * (row // 8) + row % 2
    fine = np.repeat(np.stack([fine, fine + 2], axis=1), LANES, axis=1)
    twist = 2 * np.pi * (fine * np.tile(f + shift, 2)[None, :] % NFFT) / NFFT
    out_row = np.arange(GROUP_ROWS)
    group, out_round = out_row // ROUNDS, out_row % ROUNDS
    in_row = np.arange(SHARES * 8)
    in_fine = 4 * (in_row // 8 % 16) + 2 * (in_row // 128) + in_row % 2
    in_round = in_row // 2 % ROUNDS
    last = 2 * np.pi * (in_fine[None, :] * (group - base)[:, None] % 64) / 64
    keep = (out_round[:, None] == in_round[None, :]) & (group < GROUPS)[:, None]
    scale = 2.0 / math.sqrt(WINDOWS * COARSE * LANES)
    cos_hi, cos_lo = split_bf16(np.where(keep, np.cos(last) * scale, 0.0))
    sin_hi, sin_lo = split_bf16(np.where(keep, -np.sin(last) * scale, 0.0))
    return (
        first,
        np.cos(twist).astype(np.float32),
        np.sin(twist).astype(np.float32),
        np.stack([cos_hi, cos_lo, sin_hi, sin_lo]),
    )


def whiten_kernel(spectra_ref, out_ref, rows_ref):
    for station in range(STATIONS_HERE):
        for coarse in range(COARSE):
            rows_ref[pl.ds(coarse * 8 + station * 2, 2), :] = spectra_ref[
                0, station, :, pl.ds(coarse * LANES, LANES)
            ]
    even = lax.broadcasted_iota(jnp.int32, (8, LANES), 0) % 2 == 0
    power, total = [], None
    for coarse in range(COARSE):
        value = rows_ref[pl.ds(coarse * 8, 8), :]
        square = value * value
        other = jnp.where(even, pltpu.roll(square, 7, 0), pltpu.roll(square, 1, 0))
        power.append(square + other)
        total = power[-1] if total is None else total + power[-1]
    level = jnp.sum(total, axis=1, keepdims=True) * (1.0 / (COARSE * LANES))
    water = 0.05 * (level + 1e-06)
    white = [
        rows_ref[pl.ds(coarse * 8, 8), :] * lax.rsqrt(power[coarse] + water)
        for coarse in range(COARSE)
    ]
    turned = jnp.concatenate(white, axis=0).T.astype(jnp.bfloat16)
    for copy in range(out_ref.shape[0]):
        out_ref[copy] = turned


def cross_kernel(mask_ref, home_ref, all_ref, own_table, far_table, out_ref, far_ref, left, right):
    home = home_ref[0]
    own = all_ref[pl.ds(pl.multiple_of(home * 128, 128), 128), :]
    left[...] = jnp.dot(own, own_table[...], preferred_element_type=jnp.float32)
    for r in range(ROUNDS):
        mask = mask_ref[r]
        high = (home ^ (mask >> 3)) & 7
        for block in range(8):
            other = (block ^ mask) & 7
            start = pl.multiple_of(high * 128 + other * 16, 16)
            far_ref[pl.ds(r * 128 + block * 16, 16), :] = all_ref[pl.ds(start, 16), :]
    right[...] = jnp.dot(far_ref[...], far_table[...], preferred_element_type=jnp.float32)
    sublane = lax.broadcasted_iota(jnp.int32, (8, LANES), 0)
    odd_round = sublane // 2 % 2 == 1
    lower = lax.broadcasted_iota(jnp.int32, (8, LANES), 1) < PAIR_LANES

    for block in range(8):
        for i in range(STATIONS_HERE):
            straight = crossed = None
            for r in range(ROUNDS):
                total = None
                for step in range(2):
                    rows = pl.ds(block * 16 + step * 8, 8)
                    far_rows = pl.ds(r * 128 + block * 16 + step * 8, 8)
                    for part in range(2):
                        term = (
                            left[rows, pl.ds((part * 4 + i) * LANES, LANES)]
                            * right[far_rows, pl.ds(part * LANES, LANES)]
                        )
                        total = term if total is None else total + term
                total = total + pltpu.roll(total, 4, 0)
                moved = pltpu.roll(total, 2, 0)
                straight = total if r == 0 else jnp.where(sublane >= 2 * r, total, straight)
                crossed = moved if r == 0 else jnp.where(sublane >= 2 * r, moved, crossed)
            first = jnp.where(odd_round, crossed, straight)
            second = jnp.where(odd_round, straight, crossed)
            slot = block * 8 + i * 2
            out_ref[slot] = jnp.where(
                lower, first, pltpu.roll(second, PAIR_LANES, 1)
            ).astype(jnp.bfloat16)
            out_ref[slot + 1] = jnp.where(
                lower, pltpu.roll(first, PAIR_LANES, 1), second
            ).astype(jnp.bfloat16)


def split_value(value):
    high = value.astype(jnp.bfloat16)
    return high, (value - high.astype(jnp.float32)).astype(jnp.bfloat16)


def transform_kernel(spec_ref, first_ref, cos_ref, sin_ref, last_ref, out_ref, mid_ref):
    both = spec_ref[...].astype(jnp.float32).reshape(SHARES, 2, 8, LANES)
    spec = both[:, 0] + both[:, 1]
    share = lax.broadcasted_iota(jnp.int32, spec.shape, 0)
    row = lax.broadcasted_iota(jnp.int32, spec.shape, 1)
    lane = lax.broadcasted_iota(jnp.int32, spec.shape, 2)
    zero_bin = (share == 0) & (row % 2 == 0) & (lane < 4)
    spec = jnp.where(zero_bin, 0.5 * spec, spec).reshape(SHARES * 8, LANES)
    high, low = split_value(spec)
    mid_ref[...] = jnp.dot(
        jnp.concatenate([high, low, high], axis=1),
        first_ref[...],
        preferred_element_type=jnp.float32,
    )
    half = SHARES * 4
    real, imag = [], []
    for pair in range(2):
        column_re, column_im = [], []
        for bit in range(2):
            parts_re, parts_im = [], []
            for side in range(2):
                rows = pl.ds(side * half, half)
                y_re = mid_ref[rows, pl.ds((bit * 4 + pair * 2) * LANES, LANES)]
                y_im = mid_ref[rows, pl.ds((bit * 4 + pair * 2 + 1) * LANES, LANES)]
                c = cos_ref[rows, pl.ds(bit * LANES, LANES)]
                s = sin_ref[rows, pl.ds(bit * LANES, LANES)]
                parts_re.append(y_re * c - y_im * s)
                parts_im.append(y_re * s + y_im * c)
            column_re.append(parts_re[0] + parts_re[1])
            column_im.append(parts_im[0] + parts_im[1])
        real.append(jnp.concatenate(column_re, axis=0))
        imag.append(jnp.concatenate(column_im, axis=0))
    total = None
    for index, value in ((0, jnp.concatenate(real, axis=1)), (2, jnp.concatenate(imag, axis=1))):
        high, low = split_value(value)
        for table, operand in ((index, high), (index + 1, high), (index, low)):
            term = jnp.dot(last_ref[table], operand, preferred_element_type=jnp.float32)
            total = term if total is None else total + term
    lags = out_ref.shape[2]
    for pair in range(2):
        for group in range(GROUPS):
            width = min(LANES, lags - group * LANES)
            out_ref[pair, :, pl.ds(group * LANES, width)] = total[
                group * ROUNDS : (group + 1) * ROUNDS, pair * LANES : pair * LANES + width
            ]


def spec_of(space):
    return pl.BlockSpec(memory_space=space)


def in_vmem(array):
    return pltpu.with_memory_space_constraint(jnp.asarray(array), VMEM)


def whiten(spectra, copies):
    return pl.pallas_call(
        whiten_kernel,
        out_shape=pltpu.VMEM((copies, LANES, LANES), jnp.bfloat16),
        in_specs=[spec_of(VMEM)],
        out_specs=spec_of(VMEM),
        scratch_shapes=[pltpu.VMEM((LANES, LANES), jnp.float32)],
        name="whiten",
        interpret=INTERPRET,
    )(spectra)


def cross(partner_masks, home, gathered):
    own_table, far_table = selection_tables()
    return pl.pallas_call(
        cross_kernel,
        out_shape=pltpu.VMEM((SLOTS, 8, LANES), jnp.bfloat16),
        in_specs=[spec_of(SMEM)] * 2 + [spec_of(VMEM)] * 3,
        out_specs=spec_of(VMEM),
        scratch_shapes=[
            pltpu.VMEM((512, LANES), jnp.bfloat16),
            pltpu.VMEM((LANES, 1024), jnp.float32),
            pltpu.VMEM((512, 256), jnp.float32),
        ],
        name="cross",
        interpret=INTERPRET,
    )(partner_masks, home, *map(in_vmem, (gathered, own_table, far_table)))


def transform(spec_rows):
    return pl.pallas_call(
        transform_kernel,
        out_shape=jax.ShapeDtypeStruct((2, ROUNDS, 2 * MAXLAG), jnp.float32),
        in_specs=[spec_of(VMEM)] * 5,
        out_specs=spec_of(VMEM),
        scratch_shapes=[pltpu.VMEM((SHARES * 8, 1024), jnp.float32)],
        name="transform",
        interpret=INTERPRET,
    )(*map(in_vmem, (spec_rows, *transform_tables())))


def body(spectra, partner_masks):
    rows = whiten(spectra, lax.axis_size("high"))
    gathered = lax.all_to_all(
        rows.reshape(256, 4, LANES), ("high", "low", "near"), 0, 0, tiled=True
    )
    home = lax.axis_index("high").astype(jnp.int32).reshape(1)
    spec = cross(partner_masks, home, gathered.reshape(1024, LANES))
    owned = lax.all_to_all(spec, ("low", "near", "core"), 0, 0, tiled=True)
    return transform(owned.reshape(SLOTS * 8, LANES))


def solution(mesh):
    devices = mesh.devices
    fine = Mesh(
        devices.reshape(8, devices.shape[0] // 8, devices.shape[1] // 2, 2),
        ("high", "low", "near", "core"),
    )
    return jax.shard_map(
        body,
        mesh=fine,
        in_specs=(P(("near", "core"), ("high", "low"), None, None), P()),
        out_specs=P(("high", "low", "near", "core"), None, None),
        check_vma=False,
    )
```

```python
import functools
import math

import jax
import jax.numpy as jnp
import numpy as np
from jax import lax
from jax.experimental import pallas as pl
from jax.experimental.pallas import tpu as pltpu
from jax.sharding import Mesh, PartitionSpec as P

NFFT = 8192
MAXLAG = 1200
LANES = 128
STATIONS_HERE = 4
ROUNDS = 4
WINDOWS = 8
COARSE = 16
SHARES = 32
SLOTS = 64
PAIR_LANES = 64
GROUPS = 19
GROUP_ROWS = 80
INTERPRET = False

VMEM = pltpu.MemorySpace.VMEM
SMEM = pltpu.MemorySpace.SMEM


def split_bf16(table):
    high = table.astype(jnp.bfloat16)
    low = (table - high.astype(np.float64)).astype(jnp.bfloat16)
    return high, low


@functools.lru_cache(None)
def selection_tables():
    lane = np.arange(LANES)
    coarse, station, part = lane // 8, lane // 2 % 4, lane % 2
    half, out_coarse, low, out_part = lane // 64, lane // 4 % 16, lane // 2 % 2, lane % 2
    same_bin = coarse[:, None] == out_coarse[None, :]
    own = [
        same_bin & (station == i)[:, None] & (part == c)[:, None]
        for c in range(2)
        for i in range(STATIONS_HERE)
    ]
    far_station = same_bin & (station[:, None] == (2 * half + low)[None, :])
    match = (part[:, None] == out_part[None, :]) & far_station
    cross = (part[:, None] != out_part[None, :]) & far_station
    sign = np.where(out_part == 1, -1.0, 1.0)
    return (
        np.concatenate(own, axis=1).astype(jnp.bfloat16),
        np.concatenate([match * sign, cross * 1.0], axis=1).astype(jnp.bfloat16),
    )


@functools.lru_cache(None)
def transform_tables():
    f = np.arange(LANES)
    shift = -MAXLAG % LANES
    base = (MAXLAG + shift) // LANES
    lane = np.arange(LANES)
    in_bit, coarse, pair, part = lane // 64, lane // 4 % 16, lane // 2 % 2, lane % 2
    angle = 2 * np.pi * (coarse[:, None] * (f + shift)[None, :] % 64) / 64
    cos, sin = np.cos(angle), np.sin(angle)
    real = np.where(part[:, None] == 0, cos, -sin)
    imag = np.where(part[:, None] == 0, sin, cos)
    first = np.concatenate(
        [
            np.where(((pair == p) & (in_bit == bit))[:, None], value, 0.0)
            for bit in range(2)
            for p in range(2)
            for value in (real, imag)
        ],
        axis=1,
    )
    first_hi, first_lo = split_bf16(first)
    first = np.concatenate([first_hi, first_hi, first_lo], axis=0)
    row = np.arange(SHARES * 8)
    fine = 4 * (row // 8) + row % 2
    fine = np.repeat(np.stack([fine, fine + 2], axis=1), LANES, axis=1)
    twist = 2 * np.pi * (fine * np.tile(f + shift, 2)[None, :] % NFFT) / NFFT
    out_row = np.arange(GROUP_ROWS)
    group, out_round = out_row // ROUNDS, out_row % ROUNDS
    in_row = np.arange(SHARES * 8)
    in_fine = 4 * (in_row // 8 % 16) + 2 * (in_row // 128) + in_row % 2
    in_round = in_row // 2 % ROUNDS
    last = 2 * np.pi * (in_fine[None, :] * (group - base)[:, None] % 64) / 64
    keep = (out_round[:, None] == in_round[None, :]) & (group < GROUPS)[:, None]
    scale = 2.0 / math.sqrt(WINDOWS * COARSE * LANES)
    cos_hi, cos_lo = split_bf16(np.where(keep, np.cos(last) * scale, 0.0))
    sin_hi, sin_lo = split_bf16(np.where(keep, -np.sin(last) * scale, 0.0))
    return (
        first,
        np.cos(twist).astype(np.float32),
        np.sin(twist).astype(np.float32),
        np.stack([cos_hi, cos_lo, sin_hi, sin_lo]),
    )


def whiten_kernel(spectra_ref, out_ref, rows_ref):
    for station in range(STATIONS_HERE):
        for coarse in range(COARSE):
            rows_ref[pl.ds(coarse * 8 + station * 2, 2), :] = spectra_ref[
                0, station, :, pl.ds(coarse * LANES, LANES)
            ]
    even = lax.broadcasted_iota(jnp.int32, (8, LANES), 0) % 2 == 0
    power, total = [], None
    for coarse in range(COARSE):
        value = rows_ref[pl.ds(coarse * 8, 8), :]
        square = value * value
        other = jnp.where(even, pltpu.roll(square, 7, 0), pltpu.roll(square, 1, 0))
        power.append(square + other)
        total = power[-1] if total is None else total + power[-1]
    level = jnp.sum(total, axis=1, keepdims=True) * (1.0 / (COARSE * LANES))
    water = 0.05 * (level + 1e-06)
    white = [
        rows_ref[pl.ds(coarse * 8, 8), :] * lax.rsqrt(power[coarse] + water)
        for coarse in range(COARSE)
    ]
    turned = jnp.concatenate(white, axis=0).T.astype(jnp.bfloat16)
    for copy in range(out_ref.shape[0]):
        out_ref[copy] = turned


def cross_kernel(mask_ref, all_ref, own_table, far_table, out_ref, far_ref, left, right):
    home = lax.axis_index("high")
    own = all_ref[pl.ds(pl.multiple_of(home * 128, 128), 128), :]
    left[...] = jnp.dot(own, own_table[...], preferred_element_type=jnp.float32)
    for r in range(ROUNDS):
        mask = mask_ref[r]
        high = (home ^ (mask >> 3)) & 7
        for block in range(8):
            other = (block ^ mask) & 7
            start = pl.multiple_of(high * 128 + other * 16, 16)
            far_ref[pl.ds(r * 128 + block * 16, 16), :] = all_ref[pl.ds(start, 16), :]
    right[...] = jnp.dot(far_ref[...], far_table[...], preferred_element_type=jnp.float32)
    sublane = lax.broadcasted_iota(jnp.int32, (8, LANES), 0)
    odd_round = sublane // 2 % 2 == 1
    lower = lax.broadcasted_iota(jnp.int32, (8, LANES), 1) < PAIR_LANES

    for block in range(8):
        for i in range(STATIONS_HERE):
            straight = crossed = None
            for r in range(ROUNDS):
                total = None
                for step in range(2):
                    rows = pl.ds(block * 16 + step * 8, 8)
                    far_rows = pl.ds(r * 128 + block * 16 + step * 8, 8)
                    for part in range(2):
                        term = (
                            left[rows, pl.ds((part * 4 + i) * LANES, LANES)]
                            * right[far_rows, pl.ds(part * LANES, LANES)]
                        )
                        total = term if total is None else total + term
                total = total + pltpu.roll(total, 4, 0)
                moved = pltpu.roll(total, 2, 0)
                straight = total if r == 0 else jnp.where(sublane >= 2 * r, total, straight)
                crossed = moved if r == 0 else jnp.where(sublane >= 2 * r, moved, crossed)
            first = jnp.where(odd_round, crossed, straight)
            second = jnp.where(odd_round, straight, crossed)
            slot = block * 8 + i * 2
            out_ref[slot] = jnp.where(
                lower, first, pltpu.roll(second, PAIR_LANES, 1)
            ).astype(jnp.bfloat16)
            out_ref[slot + 1] = jnp.where(
                lower, pltpu.roll(first, PAIR_LANES, 1), second
            ).astype(jnp.bfloat16)


def split_value(value):
    high = value.astype(jnp.bfloat16)
    return high, (value - high.astype(jnp.float32)).astype(jnp.bfloat16)


def transform_kernel(spec_ref, first_ref, cos_ref, sin_ref, last_ref, out_ref, mid_ref):
    both = spec_ref[...].astype(jnp.float32).reshape(SHARES, 2, 8, LANES)
    spec = both[:, 0] + both[:, 1]
    share = lax.broadcasted_iota(jnp.int32, spec.shape, 0)
    row = lax.broadcasted_iota(jnp.int32, spec.shape, 1)
    lane = lax.broadcasted_iota(jnp.int32, spec.shape, 2)
    zero_bin = (share == 0) & (row % 2 == 0) & (lane < 4)
    spec = jnp.where(zero_bin, 0.5 * spec, spec).reshape(SHARES * 8, LANES)
    high, low = split_value(spec)
    mid_ref[...] = jnp.dot(
        jnp.concatenate([high, low, high], axis=1),
        first_ref[...],
        preferred_element_type=jnp.float32,
    )
    half = SHARES * 4
    real, imag = [], []
    for pair in range(2):
        column_re, column_im = [], []
        for bit in range(2):
            parts_re, parts_im = [], []
            for side in range(2):
                rows = pl.ds(side * half, half)
                y_re = mid_ref[rows, pl.ds((bit * 4 + pair * 2) * LANES, LANES)]
                y_im = mid_ref[rows, pl.ds((bit * 4 + pair * 2 + 1) * LANES, LANES)]
                c = cos_ref[rows, pl.ds(bit * LANES, LANES)]
                s = sin_ref[rows, pl.ds(bit * LANES, LANES)]
                parts_re.append(y_re * c - y_im * s)
                parts_im.append(y_re * s + y_im * c)
            column_re.append(parts_re[0] + parts_re[1])
            column_im.append(parts_im[0] + parts_im[1])
        real.append(jnp.concatenate(column_re, axis=0))
        imag.append(jnp.concatenate(column_im, axis=0))
    total = None
    for index, value in ((0, jnp.concatenate(real, axis=1)), (2, jnp.concatenate(imag, axis=1))):
        high, low = split_value(value)
        for table, operand in ((index, high), (index + 1, high), (index, low)):
            term = jnp.dot(last_ref[table], operand, preferred_element_type=jnp.float32)
            total = term if total is None else total + term
    lags = out_ref.shape[2]
    for pair in range(2):
        for group in range(GROUPS):
            width = min(LANES, lags - group * LANES)
            out_ref[pair, :, pl.ds(group * LANES, width)] = total[
                group * ROUNDS : (group + 1) * ROUNDS, pair * LANES : pair * LANES + width
            ]


def spec_of(space):
    return pl.BlockSpec(memory_space=space)


def in_vmem(array):
    return pltpu.with_memory_space_constraint(jnp.asarray(array), VMEM)


def whiten(spectra, copies):
    return pl.pallas_call(
        whiten_kernel,
        out_shape=pltpu.VMEM((copies, LANES, LANES), jnp.bfloat16),
        in_specs=[spec_of(VMEM)],
        out_specs=spec_of(VMEM),
        scratch_shapes=[pltpu.VMEM((LANES, LANES), jnp.float32)],
        name="whiten",
        interpret=INTERPRET,
    )(spectra)


def cross(partner_masks, gathered):
    own_table, far_table = selection_tables()
    return pl.pallas_call(
        cross_kernel,
        out_shape=pltpu.VMEM((SLOTS, 8, LANES), jnp.bfloat16),
        in_specs=[spec_of(SMEM)] + [spec_of(VMEM)] * 3,
        out_specs=spec_of(VMEM),
        scratch_shapes=[
            pltpu.VMEM((512, LANES), jnp.bfloat16),
            pltpu.VMEM((LANES, 1024), jnp.float32),
            pltpu.VMEM((512, 256), jnp.float32),
        ],
        name="cross",
        interpret=INTERPRET,
    )(pltpu.with_memory_space_constraint(partner_masks, SMEM), *map(in_vmem, (gathered, own_table, far_table)))


def transform(spec_rows):
    return pl.pallas_call(
        transform_kernel,
        out_shape=jax.ShapeDtypeStruct((2, ROUNDS, 2 * MAXLAG), jnp.float32),
        in_specs=[spec_of(VMEM)] * 5,
        out_specs=spec_of(VMEM),
        scratch_shapes=[pltpu.VMEM((SHARES * 8, 1024), jnp.float32)],
        name="transform",
        interpret=INTERPRET,
    )(*map(in_vmem, (spec_rows, *transform_tables())))


def body(spectra, partner_masks):
    rows = whiten(spectra, lax.axis_size("high"))
    gathered = lax.all_to_all(
        rows.reshape(256, 4, LANES), ("high", "low", "near"), 0, 0, tiled=True
    )
    spec = cross(partner_masks, gathered.reshape(1024, LANES))
    owned = lax.all_to_all(spec, ("low", "near", "core"), 0, 0, tiled=True)
    return transform(owned.reshape(SLOTS * 8, LANES))


def solution(mesh):
    devices = mesh.devices
    fine = Mesh(
        devices.reshape(8, devices.shape[0] // 8, devices.shape[1] // 2, 2),
        ("high", "low", "near", "core"),
    )
    return jax.shard_map(
        body,
        mesh=fine,
        in_specs=(P(("near", "core"), ("high", "low"), None, None), P()),
        out_specs=P(("high", "low", "near", "core"), None, None),
        check_vma=False,
    )
```

```python
import functools
import math

import jax
import jax.numpy as jnp
import numpy as np
from jax import lax
from jax.experimental import pallas as pl
from jax.experimental.pallas import tpu as pltpu
from jax.sharding import Mesh, PartitionSpec as P

NFFT = 8192
MAXLAG = 1200
LANES = 128
STATIONS_HERE = 4
ROUNDS = 4
WINDOWS = 8
COARSE = 16
SHARES = 32
SLOTS = 64
PAIR_LANES = 64
GROUPS = 19
GROUP_ROWS = 80
INTERPRET = False

VMEM = pltpu.MemorySpace.VMEM


def split_bf16(table):
    high = table.astype(jnp.bfloat16)
    low = (table - high.astype(np.float64)).astype(jnp.bfloat16)
    return high, low


@functools.lru_cache(None)
def selection_tables():
    lane = np.arange(LANES)
    coarse, station, part = lane // 8, lane // 2 % 4, lane % 2
    half, out_coarse, low, out_part = lane // 64, lane // 4 % 16, lane // 2 % 2, lane % 2
    same_bin = coarse[:, None] == out_coarse[None, :]
    own = [
        same_bin & (station == i)[:, None] & (part == c)[:, None]
        for c in range(2)
        for i in range(STATIONS_HERE)
    ]
    far_station = same_bin & (station[:, None] == (2 * half + low)[None, :])
    match = (part[:, None] == out_part[None, :]) & far_station
    cross = (part[:, None] != out_part[None, :]) & far_station
    sign = np.where(out_part == 1, -1.0, 1.0)
    return (
        np.concatenate(own, axis=1).astype(jnp.bfloat16),
        np.concatenate([match * sign, cross * 1.0], axis=1).astype(jnp.bfloat16),
    )


@functools.lru_cache(None)
def transform_tables():
    f = np.arange(LANES)
    shift = -MAXLAG % LANES
    base = (MAXLAG + shift) // LANES
    lane = np.arange(LANES)
    in_bit, coarse, pair, part = lane // 64, lane // 4 % 16, lane // 2 % 2, lane % 2
    angle = 2 * np.pi * (coarse[:, None] * (f + shift)[None, :] % 64) / 64
    cos, sin = np.cos(angle), np.sin(angle)
    real = np.where(part[:, None] == 0, cos, -sin)
    imag = np.where(part[:, None] == 0, sin, cos)
    first = np.concatenate(
        [
            np.where(((pair == p) & (in_bit == bit))[:, None], value, 0.0)
            for bit in range(2)
            for p in range(2)
            for value in (real, imag)
        ],
        axis=1,
    )
    first_hi, first_lo = split_bf16(first)
    first = np.concatenate([first_hi, first_hi, first_lo], axis=0)
    row = np.arange(SHARES * 8)
    fine = 4 * (row // 8) + row % 2
    fine = np.repeat(np.stack([fine, fine + 2], axis=1), LANES, axis=1)
    twist = 2 * np.pi * (fine * np.tile(f + shift, 2)[None, :] % NFFT) / NFFT
    out_row = np.arange(GROUP_ROWS)
    group, out_round = out_row // ROUNDS, out_row % ROUNDS
    in_row = np.arange(SHARES * 8)
    in_fine = 4 * (in_row // 8 % 16) + 2 * (in_row // 128) + in_row % 2
    in_round = in_row // 2 % ROUNDS
    last = 2 * np.pi * (in_fine[None, :] * (group - base)[:, None] % 64) / 64
    keep = (out_round[:, None] == in_round[None, :]) & (group < GROUPS)[:, None]
    scale = 2.0 / math.sqrt(WINDOWS * COARSE * LANES)
    cos_hi, cos_lo = split_bf16(np.where(keep, np.cos(last) * scale, 0.0))
    sin_hi, sin_lo = split_bf16(np.where(keep, -np.sin(last) * scale, 0.0))
    return (
        first,
        np.cos(twist).astype(np.float32),
        np.sin(twist).astype(np.float32),
        np.stack([cos_hi, cos_lo, sin_hi, sin_lo]),
    )


def whiten_kernel(spectra_ref, out_ref, rows_ref):
    for station in range(STATIONS_HERE):
        for coarse in range(COARSE):
            rows_ref[pl.ds(coarse * 8 + station * 2, 2), :] = spectra_ref[
                0, station, :, pl.ds(coarse * LANES, LANES)
            ]
    even = lax.broadcasted_iota(jnp.int32, (8, LANES), 0) % 2 == 0
    power, total = [], None
    for coarse in range(COARSE):
        value = rows_ref[pl.ds(coarse * 8, 8), :]
        square = value * value
        other = jnp.where(even, pltpu.roll(square, 7, 0), pltpu.roll(square, 1, 0))
        power.append(square + other)
        total = power[-1] if total is None else total + power[-1]
    level = jnp.sum(total, axis=1, keepdims=True) * (1.0 / (COARSE * LANES))
    water = 0.05 * (level + 1e-06)
    white = [
        rows_ref[pl.ds(coarse * 8, 8), :] * lax.rsqrt(power[coarse] + water)
        for coarse in range(COARSE)
    ]
    turned = jnp.concatenate(white, axis=0).T.astype(jnp.bfloat16)
    for copy in range(out_ref.shape[0]):
        out_ref[copy] = turned


def cross_kernel(mask_hbm, all_ref, own_table, far_table, out_ref, left, right, masks, sem):
    fetch = pltpu.make_async_copy(mask_hbm, masks, sem)
    fetch.start()
    home = lax.axis_index("high")
    own = all_ref[pl.ds(pl.multiple_of(home * 128, 128), 128), :]
    left[...] = jnp.dot(own, own_table[...], preferred_element_type=jnp.float32)
    right[...] = jnp.dot(all_ref[...], far_table[...], preferred_element_type=jnp.float32)
    fetch.wait()
    far = [((home ^ (masks[r] >> 3)) & 7) * 128 for r in range(ROUNDS)]
    low = [masks[r] & 7 for r in range(ROUNDS)]
    sublane = lax.broadcasted_iota(jnp.int32, (8, LANES), 0)
    odd_round = sublane // 2 % 2 == 1
    lower = lax.broadcasted_iota(jnp.int32, (8, LANES), 1) < PAIR_LANES

    for block in range(8):
        starts = [far[r] + (block ^ low[r]) * 16 for r in range(ROUNDS)]
        for i in range(STATIONS_HERE):
            straight = crossed = None
            for r in range(ROUNDS):
                total = None
                for step in range(2):
                    rows = pl.ds(block * 16 + step * 8, 8)
                    far_rows = pl.ds(pl.multiple_of(starts[r] + step * 8, 8), 8)
                    for part in range(2):
                        term = (
                            left[rows, pl.ds((part * 4 + i) * LANES, LANES)]
                            * right[far_rows, pl.ds(part * LANES, LANES)]
                        )
                        total = term if total is None else total + term
                total = total + pltpu.roll(total, 4, 0)
                moved = pltpu.roll(total, 2, 0)
                straight = total if r == 0 else jnp.where(sublane >= 2 * r, total, straight)
                crossed = moved if r == 0 else jnp.where(sublane >= 2 * r, moved, crossed)
            first = jnp.where(odd_round, crossed, straight)
            second = jnp.where(odd_round, straight, crossed)
            slot = block * 8 + i * 2
            out_ref[slot] = jnp.where(
                lower, first, pltpu.roll(second, PAIR_LANES, 1)
            ).astype(jnp.bfloat16)
            out_ref[slot + 1] = jnp.where(
                lower, pltpu.roll(first, PAIR_LANES, 1), second
            ).astype(jnp.bfloat16)


def split_value(value):
    high = value.astype(jnp.bfloat16)
    return high, (value - high.astype(jnp.float32)).astype(jnp.bfloat16)


def transform_kernel(spec_ref, first_ref, cos_ref, sin_ref, last_ref, out_ref, mid_ref):
    both = spec_ref[...].astype(jnp.float32).reshape(SHARES, 2, 8, LANES)
    spec = both[:, 0] + both[:, 1]
    share = lax.broadcasted_iota(jnp.int32, spec.shape, 0)
    row = lax.broadcasted_iota(jnp.int32, spec.shape, 1)
    lane = lax.broadcasted_iota(jnp.int32, spec.shape, 2)
    zero_bin = (share == 0) & (row % 2 == 0) & (lane < 4)
    spec = jnp.where(zero_bin, 0.5 * spec, spec).reshape(SHARES * 8, LANES)
    high, low = split_value(spec)
    mid_ref[...] = jnp.dot(
        jnp.concatenate([high, low, high], axis=1),
        first_ref[...],
        preferred_element_type=jnp.float32,
    )
    half = SHARES * 4
    real, imag = [], []
    for pair in range(2):
        column_re, column_im = [], []
        for bit in range(2):
            parts_re, parts_im = [], []
            for side in range(2):
                rows = pl.ds(side * half, half)
                y_re = mid_ref[rows, pl.ds((bit * 4 + pair * 2) * LANES, LANES)]
                y_im = mid_ref[rows, pl.ds((bit * 4 + pair * 2 + 1) * LANES, LANES)]
                c = cos_ref[rows, pl.ds(bit * LANES, LANES)]
                s = sin_ref[rows, pl.ds(bit * LANES, LANES)]
                parts_re.append(y_re * c - y_im * s)
                parts_im.append(y_re * s + y_im * c)
            column_re.append(parts_re[0] + parts_re[1])
            column_im.append(parts_im[0] + parts_im[1])
        real.append(jnp.concatenate(column_re, axis=0))
        imag.append(jnp.concatenate(column_im, axis=0))
    total = None
    for index, value in ((0, jnp.concatenate(real, axis=1)), (2, jnp.concatenate(imag, axis=1))):
        high, low = split_value(value)
        for table, operand in ((index, high), (index + 1, high), (index, low)):
            term = jnp.dot(last_ref[table], operand, preferred_element_type=jnp.float32)
            total = term if total is None else total + term
    lags = out_ref.shape[2]
    for pair in range(2):
        for group in range(GROUPS):
            width = min(LANES, lags - group * LANES)
            out_ref[pair, :, pl.ds(group * LANES, width)] = total[
                group * ROUNDS : (group + 1) * ROUNDS, pair * LANES : pair * LANES + width
            ]


def spec_of(space):
    return pl.BlockSpec(memory_space=space)


def in_vmem(array):
    return pltpu.with_memory_space_constraint(jnp.asarray(array), VMEM)


def whiten(spectra, copies):
    return pl.pallas_call(
        whiten_kernel,
        out_shape=pltpu.VMEM((copies, LANES, LANES), jnp.bfloat16),
        in_specs=[spec_of(VMEM)],
        out_specs=spec_of(VMEM),
        scratch_shapes=[pltpu.VMEM((LANES, LANES), jnp.float32)],
        name="whiten",
        interpret=INTERPRET,
    )(spectra)


def cross(partner_masks, gathered):
    own_table, far_table = selection_tables()
    return pl.pallas_call(
        cross_kernel,
        out_shape=pltpu.VMEM((SLOTS, 8, LANES), jnp.bfloat16),
        in_specs=[spec_of(pl.ANY)] + [spec_of(VMEM)] * 3,
        out_specs=spec_of(VMEM),
        scratch_shapes=[
            pltpu.VMEM((LANES, 1024), jnp.float32),
            pltpu.VMEM((1024, 256), jnp.float32),
            pltpu.SMEM((ROUNDS,), jnp.int32),
            pltpu.SemaphoreType.DMA,
        ],
        name="cross",
        interpret=INTERPRET,
    )(partner_masks, *map(in_vmem, (gathered, own_table, far_table)))


def transform(spec_rows):
    return pl.pallas_call(
        transform_kernel,
        out_shape=jax.ShapeDtypeStruct((2, ROUNDS, 2 * MAXLAG), jnp.float32),
        in_specs=[spec_of(VMEM)] * 5,
        out_specs=spec_of(VMEM),
        scratch_shapes=[pltpu.VMEM((SHARES * 8, 1024), jnp.float32)],
        name="transform",
        interpret=INTERPRET,
    )(*map(in_vmem, (spec_rows, *transform_tables())))


def body(spectra, partner_masks):
    rows = whiten(spectra, lax.axis_size("high"))
    gathered = lax.all_to_all(
        rows.reshape(256, 4, LANES), ("high", "low", "near"), 0, 0, tiled=True
    )
    spec = cross(partner_masks, gathered.reshape(1024, LANES))
    owned = lax.all_to_all(spec, ("low", "near", "core"), 0, 0, tiled=True)
    return transform(owned.reshape(SLOTS * 8, LANES))


def solution(mesh):
    devices = mesh.devices
    fine = Mesh(
        devices.reshape(8, devices.shape[0] // 8, devices.shape[1] // 2, 2),
        ("high", "low", "near", "core"),
    )
    return jax.shard_map(
        body,
        mesh=fine,
        in_specs=(P(("near", "core"), ("high", "low"), None, None), P()),
        out_specs=P(("high", "low", "near", "core"), None, None),
        check_vma=False,
    )
```

```python
import functools
import math

import jax
import jax.numpy as jnp
import numpy as np
from jax import lax
from jax.experimental import pallas as pl
from jax.experimental.pallas import tpu as pltpu
from jax.sharding import Mesh, PartitionSpec as P

NFFT = 8192
MAXLAG = 1200
LANES = 128
STATIONS_HERE = 4
ROUNDS = 4
WINDOWS = 8
COARSE = 16
SHARES = 32
SLOTS = 64
PAIR_LANES = 64
GROUPS = 19
GROUP_ROWS = 80
INTERPRET = False

VMEM = pltpu.MemorySpace.VMEM
SMEM = pltpu.MemorySpace.SMEM


def split_bf16(table):
    high = table.astype(jnp.bfloat16)
    low = (table - high.astype(np.float64)).astype(jnp.bfloat16)
    return high, low


@functools.lru_cache(None)
def selection_tables():
    lane = np.arange(LANES)
    coarse, station, part = lane // 8, lane // 2 % 4, lane % 2
    half, out_coarse, low, out_part = lane // 64, lane // 4 % 16, lane // 2 % 2, lane % 2
    same_bin = coarse[:, None] == out_coarse[None, :]
    own = [
        same_bin & (station == i)[:, None] & (part[:, None] == half[None, :])
        for i in range(STATIONS_HERE)
    ]
    far_station = same_bin & (station[:, None] == (2 * half + low)[None, :])
    match = np.where(out_part == 1, -1.0, 1.0) * (part[:, None] == out_part[None, :])
    cross = 1.0 * (part[:, None] != out_part[None, :])
    far = [far_station * np.where(half == side, match, cross) for side in range(2)]
    return (
        np.concatenate(own, axis=1).astype(jnp.bfloat16),
        np.concatenate(far, axis=1).astype(jnp.bfloat16),
    )


@functools.lru_cache(None)
def transform_tables():
    f = np.arange(LANES)
    shift = -MAXLAG % LANES
    base = (MAXLAG + shift) // LANES
    lane = np.arange(LANES)
    in_bit, coarse, pair, part = lane // 64, lane // 4 % 16, lane // 2 % 2, lane % 2
    angle = 2 * np.pi * (coarse[:, None] * (f % 64 + shift)[None, :] % 64) / 64
    angle = angle - np.where(f >= 64, np.pi / 2, 0.0)[None, :]
    turned = np.where(part[:, None] == 0, np.cos(angle), -np.sin(angle))
    first = np.concatenate(
        [
            np.where(((pair == p) & (in_bit == bit))[:, None], turned, 0.0)
            for bit in range(2)
            for p in range(2)
        ],
        axis=1,
    )
    first_hi, first_lo = split_bf16(first)
    first = np.concatenate([first_hi, first_hi, first_lo], axis=0)
    row = np.arange(SHARES * 8)
    fine = 4 * (row // 8) + row % 2
    fine = np.repeat(np.stack([fine, fine + 2], axis=1), LANES, axis=1)
    twist = 2 * np.pi * (fine * np.tile(f + shift, 2)[None, :] % NFFT) / NFFT
    cos, sin, early = np.cos(twist), np.sin(twist), np.tile(f < 64, 2)[None, :]
    twists = [
        np.where(early, cos, -sin),
        np.where(early, -sin, cos),
        np.where(early, sin, cos),
        np.where(early, cos, sin),
    ]
    out_row = np.arange(GROUP_ROWS)
    group, out_round = out_row // ROUNDS, out_row % ROUNDS
    in_row = np.arange(SHARES * 8)
    in_fine = 4 * (in_row // 8 % 16) + 2 * (in_row // 128) + in_row % 2
    in_round = in_row // 2 % ROUNDS
    last = 2 * np.pi * (in_fine[None, :] * (group - base)[:, None] % 64) / 64
    keep = (out_round[:, None] == in_round[None, :]) & (group < GROUPS)[:, None]
    scale = 2.0 / math.sqrt(WINDOWS * COARSE * LANES)
    last = np.concatenate([np.cos(last), -np.sin(last)], axis=1) * scale
    last_hi, last_lo = split_bf16(np.where(np.tile(keep, 2), last, 0.0))
    return (
        first,
        np.stack(twists).astype(np.float32),
        np.concatenate([last_hi, last_lo], axis=0),
    )


def whiten_kernel(spectra_ref, mask_ref, out_ref, mask_out, rows_ref):
    for r in range(ROUNDS):
        mask_out[r] = mask_ref[r]
    for station in range(STATIONS_HERE):
        for coarse in range(COARSE):
            rows_ref[pl.ds(coarse * 8 + station * 2, 2), :] = spectra_ref[
                0, station, :, pl.ds(coarse * LANES, LANES)
            ]
    even = lax.broadcasted_iota(jnp.int32, (8, LANES), 0) % 2 == 0
    power, total = [], None
    for coarse in range(COARSE):
        value = rows_ref[pl.ds(coarse * 8, 8), :]
        square = value * value
        other = jnp.where(even, pltpu.roll(square, 7, 0), pltpu.roll(square, 1, 0))
        power.append(square + other)
        total = power[-1] if total is None else total + power[-1]
    level = jnp.sum(total, axis=1, keepdims=True) * (1.0 / (COARSE * LANES))
    water = 0.05 * (level + 1e-06)
    white = [
        rows_ref[pl.ds(coarse * 8, 8), :] * lax.rsqrt(power[coarse] + water)
        for coarse in range(COARSE)
    ]
    turned = jnp.concatenate(white, axis=0).T.astype(jnp.bfloat16)
    for copy in range(out_ref.shape[0]):
        out_ref[copy] = turned


def cross_kernel(mask_ref, all_ref, own_table, far_table, out_ref, far_ref, left, right):
    home = lax.axis_index("high")
    own = all_ref[pl.ds(pl.multiple_of(home * 128, 128), 128), :]
    left[...] = jnp.dot(own, own_table[...], preferred_element_type=jnp.float32)
    for r in range(ROUNDS):
        mask = mask_ref[r]
        high = (home ^ (mask >> 3)) & 7
        for block in range(8):
            start = pl.multiple_of(high * 128 + ((block ^ mask) & 7) * 16, 16)
            far_ref[pl.ds(r * 128 + block * 16, 16), :] = all_ref[pl.ds(start, 16), :]
    right[...] = jnp.dot(far_ref[...], far_table[...], preferred_element_type=jnp.float32)
    sublane = lax.broadcasted_iota(jnp.int32, (8, LANES), 0)
    odd_round = sublane // 2 % 2 == 1
    lower = lax.broadcasted_iota(jnp.int32, (8, LANES), 1) < PAIR_LANES

    for block in range(8):
        for i in range(STATIONS_HERE):
            straight = crossed = None
            sides = []
            for step in range(2):
                side = left[pl.ds(block * 16 + step * 8, 8), pl.ds(i * LANES, LANES)]
                sides.append((side, pltpu.roll(side, PAIR_LANES, 1)))
            for r in range(ROUNDS):
                total = None
                for step in range(2):
                    far_rows = pl.ds(r * 128 + block * 16 + step * 8, 8)
                    for part in range(2):
                        term = sides[step][part] * right[far_rows, pl.ds(part * LANES, LANES)]
                        total = term if total is None else total + term
                total = total + pltpu.roll(total, 4, 0)
                moved = pltpu.roll(total, 2, 0)
                straight = total if r == 0 else jnp.where(sublane >= 2 * r, total, straight)
                crossed = moved if r == 0 else jnp.where(sublane >= 2 * r, moved, crossed)
            first = jnp.where(odd_round, crossed, straight)
            second = jnp.where(odd_round, straight, crossed)
            slot = block * 8 + i * 2
            out_ref[slot] = jnp.where(
                lower, first, pltpu.roll(second, PAIR_LANES, 1)
            ).astype(jnp.bfloat16)
            out_ref[slot + 1] = jnp.where(
                lower, pltpu.roll(first, PAIR_LANES, 1), second
            ).astype(jnp.bfloat16)


def split_value(value):
    high = value.astype(jnp.bfloat16)
    return high, (value - high.astype(jnp.float32)).astype(jnp.bfloat16)


def transform_kernel(spec_ref, first_ref, twist_ref, last_ref, out_ref, mid_ref, high_ref, low_ref):
    both = spec_ref[...].astype(jnp.float32).reshape(SHARES, 2, 8, LANES)
    spec = both[:, 0] + both[:, 1]
    share = lax.broadcasted_iota(jnp.int32, spec.shape, 0)
    row = lax.broadcasted_iota(jnp.int32, spec.shape, 1)
    lane = lax.broadcasted_iota(jnp.int32, spec.shape, 2)
    zero_bin = (share == 0) & (row % 2 == 0) & (lane < 4)
    spec = jnp.where(zero_bin, 0.5 * spec, spec).reshape(SHARES * 8, LANES)
    high, low = split_value(spec)
    mid_ref[...] = jnp.dot(
        jnp.concatenate([high, low, high], axis=1),
        first_ref[...],
        preferred_element_type=jnp.float32,
    )
    half = SHARES * 4
    for bit in range(2):
        for start in range(0, half, 16):
            sums = [[None, None], [None, None]]
            for side in range(2):
                rows = pl.ds(side * half + start, 16)
                twists = [twist_ref[t, rows, pl.ds(bit * LANES, LANES)] for t in range(4)]
                for pair in range(2):
                    value = mid_ref[rows, pl.ds((bit * 2 + pair) * LANES, LANES)]
                    other = pltpu.roll(value, 64, 1)
                    for part in range(2):
                        term = value * twists[2 * part] + other * twists[2 * part + 1]
                        known = sums[pair][part]
                        sums[pair][part] = term if known is None else known + term
            for pair in range(2):
                for part in range(2):
                    rows = pl.ds(part * 2 * half + bit * half + start, 16)
                    columns = pl.ds(pair * LANES, LANES)
                    high_ref[rows, columns], low_ref[rows, columns] = split_value(sums[pair][part])
    double = jnp.dot(last_ref[...], high_ref[...], preferred_element_type=jnp.float32)
    single = jnp.dot(
        last_ref[pl.ds(0, GROUP_ROWS), :], low_ref[...], preferred_element_type=jnp.float32
    )
    total = double[:GROUP_ROWS] + double[GROUP_ROWS:] + single
    lags = out_ref.shape[2]
    for pair in range(2):
        for group in range(GROUPS):
            width = min(LANES, lags - group * LANES)
            out_ref[pair, :, pl.ds(group * LANES, width)] = total[
                group * ROUNDS : (group + 1) * ROUNDS, pair * LANES : pair * LANES + width
            ]


def spec_of(space):
    return pl.BlockSpec(memory_space=space)


def in_vmem(array):
    return pltpu.with_memory_space_constraint(jnp.asarray(array), VMEM)


def whiten(spectra, partner_masks, copies):
    return pl.pallas_call(
        whiten_kernel,
        out_shape=(
            pltpu.VMEM((copies, LANES, LANES), jnp.bfloat16),
            pltpu.SMEM((ROUNDS,), jnp.int32),
        ),
        in_specs=[spec_of(VMEM), spec_of(SMEM)],
        out_specs=(spec_of(VMEM), spec_of(SMEM)),
        scratch_shapes=[pltpu.VMEM((LANES, LANES), jnp.float32)],
        name="whiten",
        interpret=INTERPRET,
    )(spectra, partner_masks)


def cross(partner_masks, gathered):
    own_table, far_table = selection_tables()
    return pl.pallas_call(
        cross_kernel,
        out_shape=pltpu.VMEM((SLOTS, 8, LANES), jnp.bfloat16),
        in_specs=[spec_of(SMEM)] + [spec_of(VMEM)] * 3,
        out_specs=spec_of(VMEM),
        scratch_shapes=[
            pltpu.VMEM((512, LANES), jnp.bfloat16),
            pltpu.VMEM((LANES, 512), jnp.float32),
            pltpu.VMEM((512, 256), jnp.float32),
        ],
        name="cross",
        interpret=INTERPRET,
    )(pltpu.with_memory_space_constraint(partner_masks, SMEM), *map(in_vmem, (gathered, own_table, far_table)))


def transform(spec_rows):
    return pl.pallas_call(
        transform_kernel,
        out_shape=jax.ShapeDtypeStruct((2, ROUNDS, 2 * MAXLAG), jnp.float32),
        in_specs=[spec_of(VMEM)] * 4,
        out_specs=spec_of(VMEM),
        scratch_shapes=[
            pltpu.VMEM((SHARES * 8, 512), jnp.float32),
            pltpu.VMEM((SHARES * 16, 256), jnp.bfloat16),
            pltpu.VMEM((SHARES * 16, 256), jnp.bfloat16),
        ],
        name="transform",
        interpret=INTERPRET,
    )(*map(in_vmem, (spec_rows, *transform_tables())))


def body(spectra, partner_masks):
    rows, masks = whiten(spectra, partner_masks, lax.axis_size("high"))
    gathered = lax.all_to_all(
        rows.reshape(256, 4, LANES), ("high", "low", "near"), 0, 0, tiled=True
    )
    spec = cross(masks, gathered.reshape(1024, LANES))
    owned = lax.all_to_all(spec, ("low", "near", "core"), 0, 0, tiled=True)
    return transform(owned.reshape(SLOTS * 8, LANES))


def solution(mesh):
    devices = mesh.devices
    fine = Mesh(
        devices.reshape(8, devices.shape[0] // 8, devices.shape[1] // 2, 2),
        ("high", "low", "near", "core"),
    )
    return jax.shard_map(
        body,
        mesh=fine,
        in_specs=(P(("near", "core"), ("high", "low"), None, None), P()),
        out_specs=P(("high", "low", "near", "core"), None, None),
        check_vma=False,
    )
```

```python
import functools
import math

import jax
import jax.numpy as jnp
import numpy as np
from jax import lax
from jax.experimental import pallas as pl
from jax.experimental.pallas import tpu as pltpu
from jax.sharding import Mesh, PartitionSpec as P

NFFT = 8192
MAXLAG = 1200
LANES = 128
STATIONS_HERE = 4
ROUNDS = 4
WINDOWS = 8
COARSE = 16
SHARES = 32
SLOTS = 64
PAIR_LANES = 64
GROUPS = 19
GROUP_ROWS = 80
INTERPRET = False

VMEM = pltpu.MemorySpace.VMEM
SMEM = pltpu.MemorySpace.SMEM


def split_bf16(table):
    high = table.astype(jnp.bfloat16)
    low = (table - high.astype(np.float64)).astype(jnp.bfloat16)
    return high, low


@functools.lru_cache(None)
def selection_tables():
    lane = np.arange(LANES)
    coarse, station, part = lane // 8, lane // 2 % 4, lane % 2
    half, out_coarse, low, out_part = lane // 64, lane // 4 % 16, lane // 2 % 2, lane % 2
    same_bin = coarse[:, None] == out_coarse[None, :]
    own = [
        same_bin & (station == i)[:, None] & (part[:, None] == half[None, :])
        for i in range(STATIONS_HERE)
    ]
    far_station = same_bin & (station[:, None] == (2 * half + low)[None, :])
    match = np.where(out_part == 1, -1.0, 1.0) * (part[:, None] == out_part[None, :])
    cross = 1.0 * (part[:, None] != out_part[None, :])
    far = [far_station * np.where(half == side, match, cross) for side in range(2)]
    return (
        np.concatenate(own, axis=1).astype(jnp.bfloat16),
        np.concatenate(far, axis=1).astype(jnp.bfloat16),
    )


@functools.lru_cache(None)
def transform_tables():
    f = np.arange(LANES)
    shift = -MAXLAG % LANES
    base = (MAXLAG + shift) // LANES
    lane = np.arange(LANES)
    in_bit, coarse, pair, part = lane // 64, lane // 4 % 16, lane // 2 % 2, lane % 2
    angle = 2 * np.pi * (coarse[:, None] * (f + shift)[None, :] % 64) / 64
    cos, sin = np.cos(angle), np.sin(angle)
    real = np.where(part[:, None] == 0, cos, -sin)
    imag = np.where(part[:, None] == 0, sin, cos)
    first = np.concatenate(
        [
            np.where(((pair == p) & (in_bit == bit))[:, None], value, 0.0)
            for bit in range(2)
            for p in range(2)
            for value in (real, imag)
        ],
        axis=1,
    )
    first_hi, first_lo = split_bf16(first)
    first = np.concatenate([first_hi, first_hi, first_lo], axis=0)
    row = np.arange(SHARES * 8)
    fine = 4 * (row // 8) + row % 2
    fine = np.repeat(np.stack([fine, fine + 2], axis=1), LANES, axis=1)
    twist = 2 * np.pi * (fine * np.tile(f + shift, 2)[None, :] % NFFT) / NFFT
    out_row = np.arange(GROUP_ROWS)
    group, out_round = out_row // ROUNDS, out_row % ROUNDS
    in_row = np.arange(SHARES * 8)
    in_fine = 4 * (in_row // 8 % 16) + 2 * (in_row // 128) + in_row % 2
    in_round = in_row // 2 % ROUNDS
    last = 2 * np.pi * (in_fine[None, :] * (group - base)[:, None] % 64) / 64
    keep = (out_round[:, None] == in_round[None, :]) & (group < GROUPS)[:, None]
    scale = 2.0 / math.sqrt(WINDOWS * COARSE * LANES)
    cos_hi, cos_lo = split_bf16(np.where(keep, np.cos(last) * scale, 0.0))
    sin_hi, sin_lo = split_bf16(np.where(keep, -np.sin(last) * scale, 0.0))
    return (
        first,
        np.cos(twist).astype(np.float32),
        np.sin(twist).astype(np.float32),
        np.stack([cos_hi, cos_lo, sin_hi, sin_lo]),
    )


def whiten_kernel(spectra_hbm, *refs):
    inputs, (out_ref, *outputs), (spectra_ref, rows_ref, sems) = refs[:4], refs[4:9], refs[9:]
    pairs = [(spectra_hbm, spectra_ref), *zip(inputs, outputs)]
    copies = [pltpu.make_async_copy(*pair, sems.at[n]) for n, pair in enumerate(pairs)]
    for copy in copies:
        copy.start()
    copies[0].wait()
    for station in range(STATIONS_HERE):
        for coarse in range(COARSE):
            rows_ref[pl.ds(coarse * 8 + station * 2, 2), :] = spectra_ref[
                0, station, :, pl.ds(coarse * LANES, LANES)
            ]
    even = lax.broadcasted_iota(jnp.int32, (8, LANES), 0) % 2 == 0
    power, total = [], None
    for coarse in range(COARSE):
        value = rows_ref[pl.ds(coarse * 8, 8), :]
        square = value * value
        other = jnp.where(even, pltpu.roll(square, 7, 0), pltpu.roll(square, 1, 0))
        power.append(square + other)
        total = power[-1] if total is None else total + power[-1]
    level = jnp.sum(total, axis=1, keepdims=True) * (1.0 / (COARSE * LANES))
    water = 0.05 * (level + 1e-06)
    white = [
        rows_ref[pl.ds(coarse * 8, 8), :] * lax.rsqrt(power[coarse] + water)
        for coarse in range(COARSE)
    ]
    turned = jnp.concatenate(white, axis=0).T.astype(jnp.bfloat16)
    for index in range(out_ref.shape[0]):
        out_ref[index] = turned
    for copy in copies[1:]:
        copy.wait()


def cross_kernel(mask_ref, all_ref, own_table, far_table, out_ref, far_ref, left, right):
    home = lax.axis_index("high")
    own = all_ref[pl.ds(pl.multiple_of(home * 128, 128), 128), :]
    left[...] = jnp.dot(own, own_table[...], preferred_element_type=jnp.float32)
    for r in range(ROUNDS):
        mask = mask_ref[r]
        high = (home ^ (mask >> 3)) & 7
        for block in range(8):
            start = pl.multiple_of(high * 128 + ((block ^ mask) & 7) * 16, 16)
            far_ref[pl.ds(r * 128 + block * 16, 16), :] = all_ref[pl.ds(start, 16), :]
    right[...] = jnp.dot(far_ref[...], far_table[...], preferred_element_type=jnp.float32)
    sublane = lax.broadcasted_iota(jnp.int32, (8, LANES), 0)
    odd_round = sublane // 2 % 2 == 1
    lower = lax.broadcasted_iota(jnp.int32, (8, LANES), 1) < PAIR_LANES

    for block in range(8):
        for i in range(STATIONS_HERE):
            straight = crossed = None
            sides = []
            for step in range(2):
                side = left[pl.ds(block * 16 + step * 8, 8), pl.ds(i * LANES, LANES)]
                sides.append((side, pltpu.roll(side, PAIR_LANES, 1)))
            for r in range(ROUNDS):
                total = None
                for step in range(2):
                    far_rows = pl.ds(r * 128 + block * 16 + step * 8, 8)
                    for part in range(2):
                        term = sides[step][part] * right[far_rows, pl.ds(part * LANES, LANES)]
                        total = term if total is None else total + term
                total = total + pltpu.roll(total, 4, 0)
                moved = pltpu.roll(total, 2, 0)
                straight = total if r == 0 else jnp.where(sublane >= 2 * r, total, straight)
                crossed = moved if r == 0 else jnp.where(sublane >= 2 * r, moved, crossed)
            first = jnp.where(odd_round, crossed, straight)
            second = jnp.where(odd_round, straight, crossed)
            slot = block * 8 + i * 2
            out_ref[slot] = jnp.where(
                lower, first, pltpu.roll(second, PAIR_LANES, 1)
            ).astype(jnp.bfloat16)
            out_ref[slot + 1] = jnp.where(
                lower, pltpu.roll(first, PAIR_LANES, 1), second
            ).astype(jnp.bfloat16)


def split_value(value):
    high = value.astype(jnp.bfloat16)
    return high, (value - high.astype(jnp.float32)).astype(jnp.bfloat16)


def transform_kernel(spec_ref, first_ref, cos_ref, sin_ref, last_ref, out_ref, mid_ref):
    both = spec_ref[...].astype(jnp.float32).reshape(SHARES, 2, 8, LANES)
    spec = both[:, 0] + both[:, 1]
    share = lax.broadcasted_iota(jnp.int32, spec.shape, 0)
    row = lax.broadcasted_iota(jnp.int32, spec.shape, 1)
    lane = lax.broadcasted_iota(jnp.int32, spec.shape, 2)
    zero_bin = (share == 0) & (row % 2 == 0) & (lane < 4)
    spec = jnp.where(zero_bin, 0.5 * spec, spec).reshape(SHARES * 8, LANES)
    high, low = split_value(spec)
    mid_ref[...] = jnp.dot(
        jnp.concatenate([high, low, high], axis=1),
        first_ref[...],
        preferred_element_type=jnp.float32,
    )
    half = SHARES * 4
    real, imag = [], []
    for pair in range(2):
        column_re, column_im = [], []
        for bit in range(2):
            parts_re, parts_im = [], []
            for side in range(2):
                rows = pl.ds(side * half, half)
                y_re = mid_ref[rows, pl.ds((bit * 4 + pair * 2) * LANES, LANES)]
                y_im = mid_ref[rows, pl.ds((bit * 4 + pair * 2 + 1) * LANES, LANES)]
                c = cos_ref[rows, pl.ds(bit * LANES, LANES)]
                s = sin_ref[rows, pl.ds(bit * LANES, LANES)]
                parts_re.append(y_re * c - y_im * s)
                parts_im.append(y_re * s + y_im * c)
            column_re.append(parts_re[0] + parts_re[1])
            column_im.append(parts_im[0] + parts_im[1])
        real.append(jnp.concatenate(column_re, axis=0))
        imag.append(jnp.concatenate(column_im, axis=0))
    total = None
    for index, value in ((0, jnp.concatenate(real, axis=1)), (2, jnp.concatenate(imag, axis=1))):
        high, low = split_value(value)
        for table, operand in ((index, high), (index + 1, high), (index, low)):
            term = jnp.dot(last_ref[table], operand, preferred_element_type=jnp.float32)
            total = term if total is None else total + term
    lags = out_ref.shape[2]
    for pair in range(2):
        for group in range(GROUPS):
            width = min(LANES, lags - group * LANES)
            out_ref[pair, :, pl.ds(group * LANES, width)] = total[
                group * ROUNDS : (group + 1) * ROUNDS, pair * LANES : pair * LANES + width
            ]


def spec_of(space):
    return pl.BlockSpec(memory_space=space)


def in_vmem(array):
    return pltpu.with_memory_space_constraint(jnp.asarray(array), VMEM)


def whiten(spectra, partner_masks, copies):
    tables = [jnp.asarray(table) for table in (*selection_tables(), transform_tables()[-1])]
    return pl.pallas_call(
        whiten_kernel,
        out_shape=(
            pltpu.VMEM((copies, LANES, LANES), jnp.bfloat16),
            pltpu.SMEM((ROUNDS,), jnp.int32),
            *[pltpu.VMEM(table.shape, table.dtype) for table in tables],
        ),
        in_specs=[spec_of(pl.ANY)] * 5,
        out_specs=(spec_of(VMEM), spec_of(SMEM), *[spec_of(VMEM)] * 3),
        scratch_shapes=[
            pltpu.VMEM(spectra.shape, jnp.float32),
            pltpu.VMEM((LANES, LANES), jnp.float32),
            pltpu.SemaphoreType.DMA((5,)),
        ],
        name="whiten",
        interpret=INTERPRET,
    )(spectra, partner_masks, *tables)


def cross(partner_masks, gathered, own_table, far_table):
    return pl.pallas_call(
        cross_kernel,
        out_shape=pltpu.VMEM((SLOTS, 8, LANES), jnp.bfloat16),
        in_specs=[spec_of(SMEM)] + [spec_of(VMEM)] * 3,
        out_specs=spec_of(VMEM),
        scratch_shapes=[
            pltpu.VMEM((512, LANES), jnp.bfloat16),
            pltpu.VMEM((LANES, 512), jnp.float32),
            pltpu.VMEM((512, 256), jnp.float32),
        ],
        name="cross",
        interpret=INTERPRET,
    )(pltpu.with_memory_space_constraint(partner_masks, SMEM), *map(in_vmem, (gathered, own_table, far_table)))


def transform(spec_rows, last_table):
    return pl.pallas_call(
        transform_kernel,
        out_shape=jax.ShapeDtypeStruct((2, ROUNDS, 2 * MAXLAG), jnp.float32),
        in_specs=[spec_of(VMEM)] * 5,
        out_specs=spec_of(VMEM),
        scratch_shapes=[pltpu.VMEM((SHARES * 8, 1024), jnp.float32)],
        name="transform",
        interpret=INTERPRET,
    )(*map(in_vmem, (spec_rows, *transform_tables()[:-1], last_table)))


def body(spectra, partner_masks):
    rows, masks, own_table, far_table, last_table = whiten(
        spectra, partner_masks, lax.axis_size("high")
    )
    gathered = lax.all_to_all(
        rows.reshape(256, 4, LANES), ("high", "low", "near"), 0, 0, tiled=True
    )
    spec = cross(masks, gathered.reshape(1024, LANES), own_table, far_table)
    owned = lax.all_to_all(spec, ("low", "near", "core"), 0, 0, tiled=True)
    return transform(owned.reshape(SLOTS * 8, LANES), last_table)


def solution(mesh):
    devices = mesh.devices
    fine = Mesh(
        devices.reshape(8, devices.shape[0] // 8, devices.shape[1] // 2, 2),
        ("high", "low", "near", "core"),
    )
    return jax.shard_map(
        body,
        mesh=fine,
        in_specs=(P(("near", "core"), ("high", "low"), None, None), P()),
        out_specs=P(("high", "low", "near", "core"), None, None),
        check_vma=False,
    )
```

```python
import functools
import math

import jax
import jax.numpy as jnp
import numpy as np
from jax import lax
from jax.experimental import pallas as pl
from jax.experimental.pallas import tpu as pltpu
from jax.sharding import Mesh, PartitionSpec as P

NFFT = 8192
MAXLAG = 1200
LANES = 128
STATIONS_HERE = 4
ROUNDS = 4
WINDOWS = 8
COARSE = 16
SHARES = 32
SLOTS = 64
PAIR_LANES = 64
GROUPS = 19
GROUP_ROWS = 80
INTERPRET = False

VMEM = pltpu.MemorySpace.VMEM
SMEM = pltpu.MemorySpace.SMEM


def split_bf16(table):
    high = table.astype(jnp.bfloat16)
    low = (table - high.astype(np.float64)).astype(jnp.bfloat16)
    return high, low


@functools.lru_cache(None)
def selection_tables():
    lane = np.arange(LANES)
    coarse, station, part = lane // 8, lane // 2 % 4, lane % 2
    half, out_coarse, low, out_part = lane // 64, lane // 4 % 16, lane // 2 % 2, lane % 2
    same_bin = coarse[:, None] == out_coarse[None, :]
    own = [
        same_bin & (station == i)[:, None] & (part[:, None] == half[None, :])
        for i in range(STATIONS_HERE)
    ]
    far_station = same_bin & (station[:, None] == (2 * half + low)[None, :])
    match = np.where(out_part == 1, -1.0, 1.0) * (part[:, None] == out_part[None, :])
    cross = 1.0 * (part[:, None] != out_part[None, :])
    far = [far_station * np.where(half == side, match, cross) for side in range(2)]
    return (
        np.concatenate(own, axis=1).astype(jnp.bfloat16),
        np.concatenate(far, axis=1).astype(jnp.bfloat16),
    )


@functools.lru_cache(None)
def transform_tables():
    f = np.arange(LANES)
    shift = -MAXLAG % LANES
    base = (MAXLAG + shift) // LANES
    lane = np.arange(LANES)
    in_bit, coarse, pair, part = lane // 64, lane // 4 % 16, lane // 2 % 2, lane % 2
    angle = 2 * np.pi * (coarse[:, None] * (f + shift)[None, :] % 64) / 64
    cos, sin = np.cos(angle), np.sin(angle)
    real = np.where(part[:, None] == 0, cos, -sin)
    imag = np.where(part[:, None] == 0, sin, cos)
    first = np.concatenate(
        [
            np.where(((pair == p) & (in_bit == bit))[:, None], value, 0.0)
            for bit in range(2)
            for p in range(2)
            for value in (real, imag)
        ],
        axis=1,
    )
    first_hi, first_lo = split_bf16(first)
    first = np.concatenate([first_hi, first_hi, first_lo], axis=0)
    row = np.arange(SHARES * 8)
    fine = 4 * (row // 8) + row % 2
    fine = np.repeat(np.stack([fine, fine + 2], axis=1), LANES, axis=1)
    twist = 2 * np.pi * (fine * np.tile(f + shift, 2)[None, :] % NFFT) / NFFT
    out_row = np.arange(GROUP_ROWS)
    group, out_round = out_row // ROUNDS, out_row % ROUNDS
    in_row = np.arange(SHARES * 8)
    in_fine = 4 * (in_row // 8 % 16) + 2 * (in_row // 128) + in_row % 2
    in_round = in_row // 2 % ROUNDS
    last = 2 * np.pi * (in_fine[None, :] * (group - base)[:, None] % 64) / 64
    keep = (out_round[:, None] == in_round[None, :]) & (group < GROUPS)[:, None]
    scale = 2.0 / math.sqrt(WINDOWS * COARSE * LANES)
    cos_hi, cos_lo = split_bf16(np.where(keep, np.cos(last) * scale, 0.0))
    sin_hi, sin_lo = split_bf16(np.where(keep, -np.sin(last) * scale, 0.0))
    return (
        first,
        np.cos(twist).astype(np.float32),
        np.sin(twist).astype(np.float32),
        np.stack([cos_hi, cos_lo, sin_hi, sin_lo]),
    )


def whiten_kernel(spectra_hbm, *refs):
    inputs, (out_ref, *outputs), (spectra_ref, rows_ref, sems) = refs[:4], refs[4:9], refs[9:]
    pairs = [(spectra_hbm.at[0, n], spectra_ref.at[n]) for n in range(STATIONS_HERE)]
    pairs += zip(inputs, outputs)
    copies = [pltpu.make_async_copy(*pair, sems.at[n]) for n, pair in enumerate(pairs)]
    for copy in copies:
        copy.start()
    for station in range(STATIONS_HERE):
        copies[station].wait()
        for coarse in range(COARSE):
            rows_ref[pl.ds(coarse * 8 + station * 2, 2), :] = spectra_ref[
                station, :, pl.ds(coarse * LANES, LANES)
            ]
    even = lax.broadcasted_iota(jnp.int32, (8, LANES), 0) % 2 == 0
    power, total = [], None
    for coarse in range(COARSE):
        value = rows_ref[pl.ds(coarse * 8, 8), :]
        square = value * value
        other = jnp.where(even, pltpu.roll(square, 7, 0), pltpu.roll(square, 1, 0))
        power.append(square + other)
        total = power[-1] if total is None else total + power[-1]
    level = jnp.sum(total, axis=1, keepdims=True) * (1.0 / (COARSE * LANES))
    water = 0.05 * (level + 1e-06)
    white = [
        rows_ref[pl.ds(coarse * 8, 8), :] * lax.rsqrt(power[coarse] + water)
        for coarse in range(COARSE)
    ]
    turned = jnp.concatenate(white, axis=0).T.astype(jnp.bfloat16)
    for index in range(out_ref.shape[0]):
        out_ref[index] = turned
    for copy in copies[STATIONS_HERE:]:
        copy.wait()


def cross_kernel(mask_ref, all_ref, own_table, far_table, out_ref, far_ref, left, right):
    home = lax.axis_index("high")
    own = all_ref[pl.ds(pl.multiple_of(home * 128, 128), 128), :]
    left[...] = jnp.dot(own, own_table[...], preferred_element_type=jnp.float32)
    for r in range(ROUNDS):
        mask = mask_ref[r]
        high = (home ^ (mask >> 3)) & 7
        for block in range(8):
            start = pl.multiple_of(high * 128 + ((block ^ mask) & 7) * 16, 16)
            far_ref[pl.ds(r * 128 + block * 16, 16), :] = all_ref[pl.ds(start, 16), :]
    right[...] = jnp.dot(far_ref[...], far_table[...], preferred_element_type=jnp.float32)
    sublane = lax.broadcasted_iota(jnp.int32, (8, LANES), 0)
    odd_round = sublane // 2 % 2 == 1
    lower = lax.broadcasted_iota(jnp.int32, (8, LANES), 1) < PAIR_LANES

    for block in range(8):
        for i in range(STATIONS_HERE):
            straight = crossed = None
            sides = []
            for step in range(2):
                side = left[pl.ds(block * 16 + step * 8, 8), pl.ds(i * LANES, LANES)]
                sides.append((side, pltpu.roll(side, PAIR_LANES, 1)))
            for r in range(ROUNDS):
                total = None
                for step in range(2):
                    far_rows = pl.ds(r * 128 + block * 16 + step * 8, 8)
                    for part in range(2):
                        term = sides[step][part] * right[far_rows, pl.ds(part * LANES, LANES)]
                        total = term if total is None else total + term
                total = total + pltpu.roll(total, 4, 0)
                moved = pltpu.roll(total, 2, 0)
                straight = total if r == 0 else jnp.where(sublane >= 2 * r, total, straight)
                crossed = moved if r == 0 else jnp.where(sublane >= 2 * r, moved, crossed)
            first = jnp.where(odd_round, crossed, straight)
            second = jnp.where(odd_round, straight, crossed)
            slot = block * 8 + i * 2
            out_ref[slot] = jnp.where(
                lower, first, pltpu.roll(second, PAIR_LANES, 1)
            ).astype(jnp.bfloat16)
            out_ref[slot + 1] = jnp.where(
                lower, pltpu.roll(first, PAIR_LANES, 1), second
            ).astype(jnp.bfloat16)


def split_value(value):
    high = value.astype(jnp.bfloat16)
    return high, (value - high.astype(jnp.float32)).astype(jnp.bfloat16)


def transform_kernel(spec_ref, first_ref, cos_ref, sin_ref, last_ref, out_hbm, mid_ref, out_ref, sems):
    both = spec_ref[...].astype(jnp.float32).reshape(SHARES, 2, 8, LANES)
    spec = both[:, 0] + both[:, 1]
    share = lax.broadcasted_iota(jnp.int32, spec.shape, 0)
    row = lax.broadcasted_iota(jnp.int32, spec.shape, 1)
    lane = lax.broadcasted_iota(jnp.int32, spec.shape, 2)
    zero_bin = (share == 0) & (row % 2 == 0) & (lane < 4)
    spec = jnp.where(zero_bin, 0.5 * spec, spec).reshape(SHARES * 8, LANES)
    high, low = split_value(spec)
    mid_ref[...] = jnp.dot(
        jnp.concatenate([high, low, high], axis=1),
        first_ref[...],
        preferred_element_type=jnp.float32,
    )
    half = SHARES * 4
    real, imag = [], []
    for pair in range(2):
        column_re, column_im = [], []
        for bit in range(2):
            parts_re, parts_im = [], []
            for side in range(2):
                rows = pl.ds(side * half, half)
                y_re = mid_ref[rows, pl.ds((bit * 4 + pair * 2) * LANES, LANES)]
                y_im = mid_ref[rows, pl.ds((bit * 4 + pair * 2 + 1) * LANES, LANES)]
                c = cos_ref[rows, pl.ds(bit * LANES, LANES)]
                s = sin_ref[rows, pl.ds(bit * LANES, LANES)]
                parts_re.append(y_re * c - y_im * s)
                parts_im.append(y_re * s + y_im * c)
            column_re.append(parts_re[0] + parts_re[1])
            column_im.append(parts_im[0] + parts_im[1])
        real.append(jnp.concatenate(column_re, axis=0))
        imag.append(jnp.concatenate(column_im, axis=0))
    total = None
    for index, value in ((0, jnp.concatenate(real, axis=1)), (2, jnp.concatenate(imag, axis=1))):
        high, low = split_value(value)
        for table, operand in ((index, high), (index + 1, high), (index, low)):
            term = jnp.dot(last_ref[table], operand, preferred_element_type=jnp.float32)
            total = term if total is None else total + term
    lags = out_ref.shape[2]
    copies = []
    for pair in range(2):
        for group in range(GROUPS):
            width = min(LANES, lags - group * LANES)
            out_ref[pair, :, pl.ds(group * LANES, width)] = total[
                group * ROUNDS : (group + 1) * ROUNDS, pair * LANES : pair * LANES + width
            ]
        copy = pltpu.make_async_copy(out_ref.at[pair], out_hbm.at[pair], sems.at[pair])
        copy.start()
        copies.append(copy)
    for copy in copies:
        copy.wait()


def spec_of(space):
    return pl.BlockSpec(memory_space=space)


def in_vmem(array):
    return pltpu.with_memory_space_constraint(jnp.asarray(array), VMEM)


def whiten(spectra, partner_masks, copies):
    tables = [jnp.asarray(table) for table in (*selection_tables(), transform_tables()[-1])]
    return pl.pallas_call(
        whiten_kernel,
        out_shape=(
            pltpu.VMEM((copies, LANES, LANES), jnp.bfloat16),
            pltpu.SMEM((ROUNDS,), jnp.int32),
            *[pltpu.VMEM(table.shape, table.dtype) for table in tables],
        ),
        in_specs=[spec_of(pl.ANY)] * 5,
        out_specs=(spec_of(VMEM), spec_of(SMEM), *[spec_of(VMEM)] * 3),
        scratch_shapes=[
            pltpu.VMEM(spectra.shape[1:], jnp.float32),
            pltpu.VMEM((LANES, LANES), jnp.float32),
            pltpu.SemaphoreType.DMA((STATIONS_HERE + 4,)),
        ],
        name="whiten",
        interpret=INTERPRET,
    )(spectra, partner_masks, *tables)


def cross(partner_masks, gathered, own_table, far_table):
    return pl.pallas_call(
        cross_kernel,
        out_shape=pltpu.VMEM((SLOTS, 8, LANES), jnp.bfloat16),
        in_specs=[spec_of(SMEM)] + [spec_of(VMEM)] * 3,
        out_specs=spec_of(VMEM),
        scratch_shapes=[
            pltpu.VMEM((512, LANES), jnp.bfloat16),
            pltpu.VMEM((LANES, 512), jnp.float32),
            pltpu.VMEM((512, 256), jnp.float32),
        ],
        name="cross",
        interpret=INTERPRET,
    )(pltpu.with_memory_space_constraint(partner_masks, SMEM), *map(in_vmem, (gathered, own_table, far_table)))


def transform(spec_rows, last_table):
    return pl.pallas_call(
        transform_kernel,
        out_shape=jax.ShapeDtypeStruct((2, ROUNDS, 2 * MAXLAG), jnp.float32),
        in_specs=[spec_of(VMEM)] * 5,
        out_specs=spec_of(pl.ANY),
        scratch_shapes=[
            pltpu.VMEM((SHARES * 8, 1024), jnp.float32),
            pltpu.VMEM((2, ROUNDS, 2 * MAXLAG), jnp.float32),
            pltpu.SemaphoreType.DMA((2,)),
        ],
        name="transform",
        interpret=INTERPRET,
    )(*map(in_vmem, (spec_rows, *transform_tables()[:-1], last_table)))


def body(spectra, partner_masks):
    rows, masks, own_table, far_table, last_table = whiten(
        spectra, partner_masks, lax.axis_size("high")
    )
    gathered = lax.all_to_all(
        rows.reshape(256, 4, LANES), ("high", "low", "near"), 0, 0, tiled=True
    )
    spec = cross(masks, gathered.reshape(1024, LANES), own_table, far_table)
    owned = lax.all_to_all(spec, ("low", "near", "core"), 0, 0, tiled=True)
    return transform(owned.reshape(SLOTS * 8, LANES), last_table)


def solution(mesh):
    devices = mesh.devices
    fine = Mesh(
        devices.reshape(8, devices.shape[0] // 8, devices.shape[1] // 2, 2),
        ("high", "low", "near", "core"),
    )
    return jax.shard_map(
        body,
        mesh=fine,
        in_specs=(P(("near", "core"), ("high", "low"), None, None), P()),
        out_specs=P(("high", "low", "near", "core"), None, None),
        check_vma=False,
    )
```

```python
import functools
import math

import jax
import jax.numpy as jnp
import numpy as np
from jax import lax
from jax.experimental import pallas as pl
from jax.experimental.pallas import tpu as pltpu
from jax.sharding import Mesh, PartitionSpec as P

NFFT = 8192
MAXLAG = 1200
LANES = 128
STATIONS_HERE = 4
ROUNDS = 4
WINDOWS = 8
COARSE = 16
SHARES = 32
SLOTS = 64
PAIR_LANES = 64
GROUPS = 19
GROUP_ROWS = 80
INTERPRET = False

VMEM = pltpu.MemorySpace.VMEM
SMEM = pltpu.MemorySpace.SMEM


def split_bf16(table):
    high = table.astype(jnp.bfloat16)
    low = (table - high.astype(np.float64)).astype(jnp.bfloat16)
    return high, low


@functools.lru_cache(None)
def selection_tables():
    lane = np.arange(LANES)
    coarse, station, part = lane // 8, lane // 2 % 4, lane % 2
    half, out_coarse, low, out_part = lane // 64, lane // 4 % 16, lane // 2 % 2, lane % 2
    same_bin = coarse[:, None] == out_coarse[None, :]
    own = [
        same_bin & (station == i)[:, None] & (part[:, None] == half[None, :])
        for i in range(STATIONS_HERE)
    ]
    far_station = same_bin & (station[:, None] == (2 * half + low)[None, :])
    match = np.where(out_part == 1, -1.0, 1.0) * (part[:, None] == out_part[None, :])
    cross = 1.0 * (part[:, None] != out_part[None, :])
    far = [far_station * np.where(half == side, match, cross) for side in range(2)]
    return (
        np.concatenate(own, axis=1).astype(jnp.bfloat16),
        np.concatenate(far, axis=1).astype(jnp.bfloat16),
    )


@functools.lru_cache(None)
def transform_tables():
    f = np.arange(LANES)
    shift = -MAXLAG % LANES
    base = (MAXLAG + shift) // LANES
    lane = np.arange(LANES)
    in_bit, coarse, pair, part = lane // 64, lane // 4 % 16, lane // 2 % 2, lane % 2
    first = []
    for side in range(2):
        steps = (2 * coarse + side)[:, None] * (f + shift)[None, :] % LANES
        cos, sin = np.cos(2 * np.pi * steps / LANES), np.sin(2 * np.pi * steps / LANES)
        real = np.where(part[:, None] == 0, cos, -sin)
        imag = np.where(part[:, None] == 0, sin, cos)
        table = np.concatenate(
            [
                np.where(((pair == p) & (in_bit == bit))[:, None], value, 0.0)
                for bit in range(2)
                for p in range(2)
                for value in (real, imag)
            ],
            axis=1,
        )
        high, low = split_bf16(table)
        first += [high, high, low]
    first = np.concatenate(first, axis=0)
    row = np.arange(SHARES * 4)
    fine = 4 * (row // 8) + row % 2
    fine = np.repeat(np.stack([fine, fine + 2], axis=1), LANES, axis=1)
    twist = 2 * np.pi * (fine * np.tile(f + shift, 2)[None, :] % NFFT) / NFFT
    out_row = np.arange(GROUP_ROWS)
    group, out_round = out_row // ROUNDS, out_row % ROUNDS
    in_row = np.arange(SHARES * 8)
    in_fine = 4 * (in_row // 8 % 16) + 2 * (in_row // 128) + in_row % 2
    in_round = in_row // 2 % ROUNDS
    last = 2 * np.pi * (in_fine[None, :] * (group - base)[:, None] % 64) / 64
    keep = (out_round[:, None] == in_round[None, :]) & (group < GROUPS)[:, None]
    scale = 2.0 / math.sqrt(WINDOWS * COARSE * LANES)
    last = np.concatenate([np.cos(last), -np.sin(last)], axis=1) * scale
    last_hi, last_lo = split_bf16(np.where(np.tile(keep, 2), last, 0.0))
    return (
        first,
        np.cos(twist).astype(np.float32),
        np.sin(twist).astype(np.float32),
        np.concatenate([last_hi, last_lo], axis=0),
    )


def whiten_kernel(spectra_hbm, *refs):
    inputs, (out_ref, *outputs), (spectra_ref, rows_ref, sems) = refs[:6], refs[6:13], refs[13:]
    pairs = [(spectra_hbm.at[0, n], spectra_ref.at[n]) for n in range(STATIONS_HERE)]
    pairs += zip(inputs, outputs)
    copies = [pltpu.make_async_copy(*pair, sems.at[n]) for n, pair in enumerate(pairs)]
    for copy in copies:
        copy.start()
    for station in range(STATIONS_HERE):
        copies[station].wait()
        for coarse in range(COARSE):
            rows_ref[pl.ds(coarse * 8 + station * 2, 2), :] = spectra_ref[
                station, :, pl.ds(coarse * LANES, LANES)
            ]
    even = lax.broadcasted_iota(jnp.int32, (8, LANES), 0) % 2 == 0
    power, total = [], None
    for coarse in range(COARSE):
        value = rows_ref[pl.ds(coarse * 8, 8), :]
        square = value * value
        other = jnp.where(even, pltpu.roll(square, 7, 0), pltpu.roll(square, 1, 0))
        power.append(square + other)
        total = power[-1] if total is None else total + power[-1]
    level = jnp.sum(total, axis=1, keepdims=True) * (1.0 / (COARSE * LANES))
    water = 0.05 * (level + 1e-06)
    white = [
        rows_ref[pl.ds(coarse * 8, 8), :] * lax.rsqrt(power[coarse] + water)
        for coarse in range(COARSE)
    ]
    turned = jnp.concatenate(white, axis=0).T.astype(jnp.bfloat16)
    for index in range(out_ref.shape[0]):
        out_ref[index] = turned
    for copy in copies[STATIONS_HERE:]:
        copy.wait()


def cross_kernel(mask_ref, all_ref, own_table, far_table, out_ref, far_ref, left, right):
    home = lax.axis_index("high")
    own = all_ref[pl.ds(pl.multiple_of(home * 128, 128), 128), :]
    left[...] = jnp.dot(own, own_table[...], preferred_element_type=jnp.float32)
    for r in range(ROUNDS):
        mask = mask_ref[r]
        high = (home ^ (mask >> 3)) & 7
        for block in range(8):
            start = pl.multiple_of(high * 128 + ((block ^ mask) & 7) * 16, 16)
            far_ref[pl.ds(r * 128 + block * 16, 16), :] = all_ref[pl.ds(start, 16), :]
    right[...] = jnp.dot(far_ref[...], far_table[...], preferred_element_type=jnp.float32)
    sublane = lax.broadcasted_iota(jnp.int32, (8, LANES), 0)
    odd_round = sublane // 2 % 2 == 1
    lower = lax.broadcasted_iota(jnp.int32, (8, LANES), 1) < PAIR_LANES

    for block in range(8):
        for i in range(STATIONS_HERE):
            straight = crossed = None
            sides = []
            for step in range(2):
                side = left[pl.ds(block * 16 + step * 8, 8), pl.ds(i * LANES, LANES)]
                sides.append((side, pltpu.roll(side, PAIR_LANES, 1)))
            for r in range(ROUNDS):
                total = None
                for step in range(2):
                    far_rows = pl.ds(r * 128 + block * 16 + step * 8, 8)
                    for part in range(2):
                        term = sides[step][part] * right[far_rows, pl.ds(part * LANES, LANES)]
                        total = term if total is None else total + term
                total = total + pltpu.roll(total, 4, 0)
                moved = pltpu.roll(total, 2, 0)
                straight = total if r == 0 else jnp.where(sublane >= 2 * r, total, straight)
                crossed = moved if r == 0 else jnp.where(sublane >= 2 * r, moved, crossed)
            first = jnp.where(odd_round, crossed, straight)
            second = jnp.where(odd_round, straight, crossed)
            slot = block * 8 + i * 2
            out_ref[slot] = jnp.where(
                lower, first, pltpu.roll(second, PAIR_LANES, 1)
            ).astype(jnp.bfloat16)
            out_ref[slot + 1] = jnp.where(
                lower, pltpu.roll(first, PAIR_LANES, 1), second
            ).astype(jnp.bfloat16)


def split_value(value):
    high = value.astype(jnp.bfloat16)
    return high, (value - high.astype(jnp.float32)).astype(jnp.bfloat16)


def transform_kernel(spec_ref, first_ref, cos_ref, sin_ref, last_ref, out_hbm, mid_ref, out_ref, sems):
    both = spec_ref[...].astype(jnp.float32).reshape(SHARES, 2, 8, LANES)
    spec = both[:, 0] + both[:, 1]
    share = lax.broadcasted_iota(jnp.int32, spec.shape, 0)
    row = lax.broadcasted_iota(jnp.int32, spec.shape, 1)
    lane = lax.broadcasted_iota(jnp.int32, spec.shape, 2)
    zero_bin = (share == 0) & (row % 2 == 0) & (lane < 4)
    spec = jnp.where(zero_bin, 0.5 * spec, spec).reshape(SHARES * 8, LANES)
    high, low = split_value(spec)
    half = SHARES * 4
    mid_ref[...] = jnp.dot(
        jnp.concatenate(
            [high[:half], low[:half], high[:half], high[half:], low[half:], high[half:]], axis=1
        ),
        first_ref[...],
        preferred_element_type=jnp.float32,
    )
    real, imag = [], []
    for pair in range(2):
        column_re, column_im = [], []
        for bit in range(2):
            y_re = mid_ref[:, pl.ds((bit * 4 + pair * 2) * LANES, LANES)]
            y_im = mid_ref[:, pl.ds((bit * 4 + pair * 2 + 1) * LANES, LANES)]
            c = cos_ref[:, pl.ds(bit * LANES, LANES)]
            s = sin_ref[:, pl.ds(bit * LANES, LANES)]
            column_re.append(y_re * c - y_im * s)
            column_im.append(y_re * s + y_im * c)
        real.append(jnp.concatenate(column_re, axis=0))
        imag.append(jnp.concatenate(column_im, axis=0))
    high, low = split_value(
        jnp.concatenate([jnp.concatenate(real, axis=1), jnp.concatenate(imag, axis=1)], axis=0)
    )
    double = jnp.dot(last_ref[...], high, preferred_element_type=jnp.float32)
    single = jnp.dot(
        last_ref[pl.ds(0, GROUP_ROWS), :], low, preferred_element_type=jnp.float32
    )
    total = double[:GROUP_ROWS] + double[GROUP_ROWS:] + single
    lags = out_ref.shape[2]
    copies = []
    for pair in range(2):
        for group in range(GROUPS):
            width = min(LANES, lags - group * LANES)
            out_ref[pair, :, pl.ds(group * LANES, width)] = total[
                group * ROUNDS : (group + 1) * ROUNDS, pair * LANES : pair * LANES + width
            ]
        copy = pltpu.make_async_copy(out_ref.at[pair], out_hbm.at[pair], sems.at[pair])
        copy.start()
        copies.append(copy)
    for copy in copies:
        copy.wait()


def spec_of(space):
    return pl.BlockSpec(memory_space=space)


def in_vmem(array):
    return pltpu.with_memory_space_constraint(jnp.asarray(array), VMEM)


def whiten(spectra, partner_masks, copies):
    tables = [jnp.asarray(table) for table in (*selection_tables(), *transform_tables()[1:])]
    return pl.pallas_call(
        whiten_kernel,
        out_shape=(
            pltpu.VMEM((copies, LANES, LANES), jnp.bfloat16),
            pltpu.SMEM((ROUNDS,), jnp.int32),
            *[pltpu.VMEM(table.shape, table.dtype) for table in tables],
        ),
        in_specs=[spec_of(pl.ANY)] * 7,
        out_specs=(spec_of(VMEM), spec_of(SMEM), *[spec_of(VMEM)] * 5),
        scratch_shapes=[
            pltpu.VMEM(spectra.shape[1:], jnp.float32),
            pltpu.VMEM((LANES, LANES), jnp.float32),
            pltpu.SemaphoreType.DMA((STATIONS_HERE + 6,)),
        ],
        name="whiten",
        interpret=INTERPRET,
    )(spectra, partner_masks, *tables)


def cross(partner_masks, gathered, own_table, far_table):
    return pl.pallas_call(
        cross_kernel,
        out_shape=pltpu.VMEM((SLOTS, 8, LANES), jnp.bfloat16),
        in_specs=[spec_of(SMEM)] + [spec_of(VMEM)] * 3,
        out_specs=spec_of(VMEM),
        scratch_shapes=[
            pltpu.VMEM((512, LANES), jnp.bfloat16),
            pltpu.VMEM((LANES, 512), jnp.float32),
            pltpu.VMEM((512, 256), jnp.float32),
        ],
        name="cross",
        interpret=INTERPRET,
    )(pltpu.with_memory_space_constraint(partner_masks, SMEM), *map(in_vmem, (gathered, own_table, far_table)))


def transform(spec_rows, *small_tables):
    return pl.pallas_call(
        transform_kernel,
        out_shape=jax.ShapeDtypeStruct((2, ROUNDS, 2 * MAXLAG), jnp.float32),
        in_specs=[spec_of(VMEM)] * 5,
        out_specs=spec_of(pl.ANY),
        scratch_shapes=[
            pltpu.VMEM((SHARES * 4, 1024), jnp.float32),
            pltpu.VMEM((2, ROUNDS, 2 * MAXLAG), jnp.float32),
            pltpu.SemaphoreType.DMA((2,)),
        ],
        name="transform",
        interpret=INTERPRET,
    )(*map(in_vmem, (spec_rows, transform_tables()[0], *small_tables)))


def body(spectra, partner_masks):
    rows, masks, own_table, far_table, *small_tables = whiten(
        spectra, partner_masks, lax.axis_size("high")
    )
    gathered = lax.all_to_all(
        rows.reshape(256, 4, LANES), ("high", "low", "near"), 0, 0, tiled=True
    )
    spec = cross(masks, gathered.reshape(1024, LANES), own_table, far_table)
    owned = lax.all_to_all(spec, ("low", "near", "core"), 0, 0, tiled=True)
    return transform(owned.reshape(SLOTS * 8, LANES), *small_tables)


def solution(mesh):
    devices = mesh.devices
    fine = Mesh(
        devices.reshape(8, devices.shape[0] // 8, devices.shape[1] // 2, 2),
        ("high", "low", "near", "core"),
    )
    return jax.shard_map(
        body,
        mesh=fine,
        in_specs=(P(("near", "core"), ("high", "low"), None, None), P()),
        out_specs=P(("high", "low", "near", "core"), None, None),
        check_vma=False,
    )
```

```python
import functools
import math

import jax
import jax.numpy as jnp
import numpy as np
from jax import lax
from jax.experimental import pallas as pl
from jax.experimental.pallas import tpu as pltpu
from jax.sharding import Mesh, PartitionSpec as P

NFFT = 8192
MAXLAG = 1200
LANES = 128
STATIONS_HERE = 4
ROUNDS = 4
WINDOWS = 8
COARSE = 16
SHARES = 32
SLOTS = 64
PAIR_LANES = 64
GROUPS = 19
GROUP_ROWS = 80
INTERPRET = False

VMEM = pltpu.MemorySpace.VMEM
SMEM = pltpu.MemorySpace.SMEM


def split_bf16(table):
    high = table.astype(jnp.bfloat16)
    low = (table - high.astype(np.float64)).astype(jnp.bfloat16)
    return high, low


@functools.lru_cache(None)
def selection_tables():
    lane = np.arange(LANES)
    coarse, station, part = lane // 8, lane // 2 % 4, lane % 2
    half, out_coarse, low, out_part = lane // 64, lane // 4 % 16, lane // 2 % 2, lane % 2
    same_bin = coarse[:, None] == out_coarse[None, :]
    own = [
        same_bin & (station == i)[:, None] & (part[:, None] == half[None, :])
        for i in range(STATIONS_HERE)
    ]
    far_station = same_bin & (station[:, None] == (2 * half + low)[None, :])
    match = np.where(out_part == 1, -1.0, 1.0) * (part[:, None] == out_part[None, :])
    cross = 1.0 * (part[:, None] != out_part[None, :])
    far = [far_station * np.where(half == side, match, cross) for side in range(2)]
    return (
        np.concatenate(own, axis=1).astype(jnp.bfloat16),
        np.concatenate(far, axis=1).astype(jnp.bfloat16),
    )


@functools.lru_cache(None)
def transform_tables():
    f = np.arange(LANES)
    shift = -MAXLAG % LANES
    base = (MAXLAG + shift) // LANES
    lane = np.arange(LANES)
    in_bit, coarse, pair, part = lane // 64, lane // 4 % 16, lane // 2 % 2, lane % 2
    first = []
    for side in range(2):
        steps = (2 * coarse + side)[:, None] * (f + shift)[None, :] % LANES
        cos, sin = np.cos(2 * np.pi * steps / LANES), np.sin(2 * np.pi * steps / LANES)
        real = np.where(part[:, None] == 0, cos, -sin)
        imag = np.where(part[:, None] == 0, sin, cos)
        table = np.concatenate(
            [
                np.where(((pair == p) & (in_bit == bit))[:, None], value, 0.0)
                for bit in range(2)
                for p in range(2)
                for value in (real, imag)
            ],
            axis=1,
        )
        high, low = split_bf16(table)
        first += [high, high, low]
    first = [np.concatenate(first[3 * side : 3 * side + 3], axis=0) for side in range(2)]
    row = np.arange(SHARES * 4)
    fine = 4 * (row // 8) + row % 2
    fine = np.repeat(np.stack([fine, fine + 2], axis=1), LANES, axis=1)
    twist = 2 * np.pi * (fine * np.tile(f + shift, 2)[None, :] % NFFT) / NFFT
    out_row = np.arange(GROUP_ROWS)
    group, out_round = out_row // ROUNDS, out_row % ROUNDS
    in_row = np.arange(SHARES * 8)
    in_fine = 4 * (in_row // 8 % 16) + 2 * (in_row // 128) + in_row % 2
    in_round = in_row // 2 % ROUNDS
    last = 2 * np.pi * (in_fine[None, :] * (group - base)[:, None] % 64) / 64
    keep = (out_round[:, None] == in_round[None, :]) & (group < GROUPS)[:, None]
    scale = 2.0 / math.sqrt(WINDOWS * COARSE * LANES)
    last = np.concatenate([np.cos(last), -np.sin(last)], axis=1) * scale
    last_hi, last_lo = split_bf16(np.where(np.tile(keep, 2), last, 0.0))
    return (
        *first,
        np.cos(twist).astype(np.float32),
        np.sin(twist).astype(np.float32),
        np.concatenate([last_hi, last_lo], axis=0),
    )


def whiten_kernel(spectra_hbm, *refs):
    inputs, (out_ref, *outputs), (spectra_ref, rows_ref, sems) = refs[:6], refs[6:13], refs[13:]
    pairs = [(spectra_hbm.at[0, n], spectra_ref.at[n]) for n in range(STATIONS_HERE)]
    pairs += zip(inputs, outputs)
    copies = [pltpu.make_async_copy(*pair, sems.at[n]) for n, pair in enumerate(pairs)]
    for copy in copies:
        copy.start()
    for station in range(STATIONS_HERE):
        copies[station].wait()
        for coarse in range(COARSE):
            rows_ref[pl.ds(coarse * 8 + station * 2, 2), :] = spectra_ref[
                station, :, pl.ds(coarse * LANES, LANES)
            ]
    even = lax.broadcasted_iota(jnp.int32, (8, LANES), 0) % 2 == 0
    power, total = [], None
    for coarse in range(COARSE):
        value = rows_ref[pl.ds(coarse * 8, 8), :]
        square = value * value
        other = jnp.where(even, pltpu.roll(square, 7, 0), pltpu.roll(square, 1, 0))
        power.append(square + other)
        total = power[-1] if total is None else total + power[-1]
    level = jnp.sum(total, axis=1, keepdims=True) * (1.0 / (COARSE * LANES))
    water = 0.05 * (level + 1e-06)
    white = [
        rows_ref[pl.ds(coarse * 8, 8), :] * lax.rsqrt(power[coarse] + water)
        for coarse in range(COARSE)
    ]
    turned = jnp.concatenate(white, axis=0).T.astype(jnp.bfloat16)
    for index in range(out_ref.shape[0]):
        out_ref[index] = turned
    for copy in copies[STATIONS_HERE:]:
        copy.wait()


def cross_kernel(mask_ref, all_ref, own_table, far_table, out_ref, far_ref, left, right):
    home = lax.axis_index("high")
    own = all_ref[pl.ds(pl.multiple_of(home * 128, 128), 128), :]
    left[...] = jnp.dot(own, own_table[...], preferred_element_type=jnp.float32)
    for r in range(ROUNDS):
        mask = mask_ref[r]
        high = (home ^ (mask >> 3)) & 7
        for block in range(8):
            start = pl.multiple_of(high * 128 + ((block ^ mask) & 7) * 16, 16)
            far_ref[pl.ds(r * 128 + block * 16, 16), :] = all_ref[pl.ds(start, 16), :]
    right[...] = jnp.dot(far_ref[...], far_table[...], preferred_element_type=jnp.float32)
    sublane = lax.broadcasted_iota(jnp.int32, (8, LANES), 0)
    odd_round = sublane // 2 % 2 == 1
    lower = lax.broadcasted_iota(jnp.int32, (8, LANES), 1) < PAIR_LANES

    for block in range(8):
        for i in range(STATIONS_HERE):
            straight = crossed = None
            sides = []
            for step in range(2):
                side = left[pl.ds(block * 16 + step * 8, 8), pl.ds(i * LANES, LANES)]
                sides.append((side, pltpu.roll(side, PAIR_LANES, 1)))
            for r in range(ROUNDS):
                total = None
                for step in range(2):
                    far_rows = pl.ds(r * 128 + block * 16 + step * 8, 8)
                    for part in range(2):
                        term = sides[step][part] * right[far_rows, pl.ds(part * LANES, LANES)]
                        total = term if total is None else total + term
                total = total + pltpu.roll(total, 4, 0)
                moved = pltpu.roll(total, 2, 0)
                straight = total if r == 0 else jnp.where(sublane >= 2 * r, total, straight)
                crossed = moved if r == 0 else jnp.where(sublane >= 2 * r, moved, crossed)
            first = jnp.where(odd_round, crossed, straight)
            second = jnp.where(odd_round, straight, crossed)
            slot = block * 8 + i * 2
            out_ref[slot] = jnp.where(
                lower, first, pltpu.roll(second, PAIR_LANES, 1)
            ).astype(jnp.bfloat16)
            out_ref[slot + 1] = jnp.where(
                lower, pltpu.roll(first, PAIR_LANES, 1), second
            ).astype(jnp.bfloat16)


def split_value(value):
    high = value.astype(jnp.bfloat16)
    return high, (value - high.astype(jnp.float32)).astype(jnp.bfloat16)


def transform_kernel(spec_ref, first_ref, second_ref, cos_ref, sin_ref, last_ref, out_hbm, mid_ref, out_ref, sems):
    both = spec_ref[...].astype(jnp.float32).reshape(SHARES, 2, 8, LANES)
    spec = both[:, 0] + both[:, 1]
    share = lax.broadcasted_iota(jnp.int32, spec.shape, 0)
    row = lax.broadcasted_iota(jnp.int32, spec.shape, 1)
    lane = lax.broadcasted_iota(jnp.int32, spec.shape, 2)
    zero_bin = (share == 0) & (row % 2 == 0) & (lane < 4)
    spec = jnp.where(zero_bin, 0.5 * spec, spec).reshape(SHARES * 8, LANES)
    high, low = split_value(spec)
    half = SHARES * 4
    mid_ref[...] = jnp.dot(
        jnp.concatenate(
            [high[:half], low[:half], high[:half], high[half:], low[half:], high[half:]], axis=1
        ),
        jnp.concatenate([first_ref[...], second_ref[...]], axis=0),
        preferred_element_type=jnp.float32,
    )
    real, imag = [], []
    for pair in range(2):
        column_re, column_im = [], []
        for bit in range(2):
            y_re = mid_ref[:, pl.ds((bit * 4 + pair * 2) * LANES, LANES)]
            y_im = mid_ref[:, pl.ds((bit * 4 + pair * 2 + 1) * LANES, LANES)]
            c = cos_ref[:, pl.ds(bit * LANES, LANES)]
            s = sin_ref[:, pl.ds(bit * LANES, LANES)]
            column_re.append(y_re * c - y_im * s)
            column_im.append(y_re * s + y_im * c)
        real.append(jnp.concatenate(column_re, axis=0))
        imag.append(jnp.concatenate(column_im, axis=0))
    high, low = split_value(
        jnp.concatenate([jnp.concatenate(real, axis=1), jnp.concatenate(imag, axis=1)], axis=0)
    )
    double = jnp.dot(last_ref[...], high, preferred_element_type=jnp.float32)
    single = jnp.dot(
        last_ref[pl.ds(0, GROUP_ROWS), :], low, preferred_element_type=jnp.float32
    )
    total = double[:GROUP_ROWS] + double[GROUP_ROWS:] + single
    lags = out_ref.shape[2]
    copies = []
    for pair in range(2):
        for group in range(GROUPS):
            width = min(LANES, lags - group * LANES)
            out_ref[pair, :, pl.ds(group * LANES, width)] = total[
                group * ROUNDS : (group + 1) * ROUNDS, pair * LANES : pair * LANES + width
            ]
        copy = pltpu.make_async_copy(out_ref.at[pair], out_hbm.at[pair], sems.at[pair])
        copy.start()
        copies.append(copy)
    for copy in copies:
        copy.wait()


def spec_of(space):
    return pl.BlockSpec(memory_space=space)


def in_vmem(array):
    return pltpu.with_memory_space_constraint(jnp.asarray(array), VMEM)


def whiten(spectra, partner_masks, copies):
    tables = [jnp.asarray(table) for table in (*selection_tables(), *transform_tables()[2:])]
    return pl.pallas_call(
        whiten_kernel,
        out_shape=(
            pltpu.VMEM((copies, LANES, LANES), jnp.bfloat16),
            pltpu.SMEM((ROUNDS,), jnp.int32),
            *[pltpu.VMEM(table.shape, table.dtype) for table in tables],
        ),
        in_specs=[spec_of(pl.ANY)] * 7,
        out_specs=(spec_of(VMEM), spec_of(SMEM), *[spec_of(VMEM)] * 5),
        scratch_shapes=[
            pltpu.VMEM(spectra.shape[1:], jnp.float32),
            pltpu.VMEM((LANES, LANES), jnp.float32),
            pltpu.SemaphoreType.DMA((STATIONS_HERE + 6,)),
        ],
        name="whiten",
        interpret=INTERPRET,
    )(spectra, partner_masks, *tables)


def cross(partner_masks, gathered, own_table, far_table):
    return pl.pallas_call(
        cross_kernel,
        out_shape=pltpu.VMEM((SLOTS, 8, LANES), jnp.bfloat16),
        in_specs=[spec_of(SMEM)] + [spec_of(VMEM)] * 3,
        out_specs=spec_of(VMEM),
        scratch_shapes=[
            pltpu.VMEM((512, LANES), jnp.bfloat16),
            pltpu.VMEM((LANES, 512), jnp.float32),
            pltpu.VMEM((512, 256), jnp.float32),
        ],
        name="cross",
        interpret=INTERPRET,
    )(pltpu.with_memory_space_constraint(partner_masks, SMEM), *map(in_vmem, (gathered, own_table, far_table)))


def transform(spec_rows, *small_tables):
    return pl.pallas_call(
        transform_kernel,
        out_shape=jax.ShapeDtypeStruct((2, ROUNDS, 2 * MAXLAG), jnp.float32),
        in_specs=[spec_of(VMEM)] * 6,
        out_specs=spec_of(pl.ANY),
        scratch_shapes=[
            pltpu.VMEM((SHARES * 4, 1024), jnp.float32),
            pltpu.VMEM((2, ROUNDS, 2 * MAXLAG), jnp.float32),
            pltpu.SemaphoreType.DMA((2,)),
        ],
        name="transform",
        interpret=INTERPRET,
    )(*map(in_vmem, (spec_rows, *transform_tables()[:2], *small_tables)))


def body(spectra, partner_masks):
    rows, masks, own_table, far_table, *small_tables = whiten(
        spectra, partner_masks, lax.axis_size("high")
    )
    gathered = lax.all_to_all(
        rows.reshape(256, 4, LANES), ("high", "low", "near"), 0, 0, tiled=True
    )
    spec = cross(masks, gathered.reshape(1024, LANES), own_table, far_table)
    owned = lax.all_to_all(spec, ("low", "near", "core"), 0, 0, tiled=True)
    return transform(owned.reshape(SLOTS * 8, LANES), *small_tables)


def solution(mesh):
    devices = mesh.devices
    fine = Mesh(
        devices.reshape(8, devices.shape[0] // 8, devices.shape[1] // 2, 2),
        ("high", "low", "near", "core"),
    )
    return jax.shard_map(
        body,
        mesh=fine,
        in_specs=(P(("near", "core"), ("high", "low"), None, None), P()),
        out_specs=P(("high", "low", "near", "core"), None, None),
        check_vma=False,
    )
```

```python
import functools
import math

import jax
import jax.numpy as jnp
import numpy as np
from jax import lax
from jax.experimental import pallas as pl
from jax.experimental.pallas import tpu as pltpu
from jax.sharding import Mesh, PartitionSpec as P

NFFT = 8192
MAXLAG = 1200
LANES = 128
STATIONS_HERE = 4
ROUNDS = 4
WINDOWS = 8
COARSE = 16
SHARES = 32
SLOTS = 64
PAIR_LANES = 64
GROUPS = 19
GROUP_ROWS = 80
INTERPRET = False

VMEM = pltpu.MemorySpace.VMEM
SMEM = pltpu.MemorySpace.SMEM


def split_bf16(table):
    high = table.astype(jnp.bfloat16)
    low = (table - high.astype(np.float64)).astype(jnp.bfloat16)
    return high, low


@functools.lru_cache(None)
def selection_tables():
    lane = np.arange(LANES)
    coarse, station, part = lane // 8, lane // 2 % 4, lane % 2
    half, out_coarse, low, out_part = lane // 64, lane // 4 % 16, lane // 2 % 2, lane % 2
    same_bin = coarse[:, None] == out_coarse[None, :]
    own = [
        same_bin & (station == i)[:, None] & (part[:, None] == half[None, :])
        for i in range(STATIONS_HERE)
    ]
    far_station = same_bin & (station[:, None] == (2 * half + low)[None, :])
    match = np.where(out_part == 1, -1.0, 1.0) * (part[:, None] == out_part[None, :])
    cross = 1.0 * (part[:, None] != out_part[None, :])
    far = [far_station * np.where(half == side, match, cross) for side in range(2)]
    return (
        np.concatenate(own, axis=1).astype(jnp.bfloat16),
        np.concatenate(far, axis=1).astype(jnp.bfloat16),
    )


@functools.lru_cache(None)
def transform_tables():
    f = np.arange(LANES)
    shift = -MAXLAG % LANES
    base = (MAXLAG + shift) // LANES
    lane = np.arange(LANES)
    in_bit, coarse, pair, part = lane // 64, lane // 4 % 16, lane // 2 % 2, lane % 2
    first = []
    for side in range(2):
        steps = (2 * coarse + side)[:, None] * (f + shift)[None, :] % LANES
        cos, sin = np.cos(2 * np.pi * steps / LANES), np.sin(2 * np.pi * steps / LANES)
        real = np.where(part[:, None] == 0, cos, -sin)
        imag = np.where(part[:, None] == 0, sin, cos)
        table = np.concatenate(
            [
                np.where(((pair == p) & (in_bit == bit))[:, None], value, 0.0)
                for bit in range(2)
                for p in range(2)
                for value in (real, imag)
            ],
            axis=1,
        )
        high, low = split_bf16(table)
        first += [high, high, low]
    first = [np.concatenate(first[3 * side : 3 * side + 3], axis=0) for side in range(2)]
    row = np.arange(SHARES * 4)
    fine = 4 * (row // 8) + row % 2
    fine = np.repeat(np.stack([fine, fine + 2], axis=1), LANES, axis=1)
    twist = 2 * np.pi * (fine * np.tile(f + shift, 2)[None, :] % NFFT) / NFFT
    out_row = np.arange(GROUP_ROWS)
    group, out_round = out_row // ROUNDS, out_row % ROUNDS
    in_row = np.arange(SHARES * 8)
    in_fine = 4 * (in_row // 8 % 16) + 2 * (in_row // 128) + in_row % 2
    in_round = in_row // 2 % ROUNDS
    last = 2 * np.pi * (in_fine[None, :] * (group - base)[:, None] % 64) / 64
    keep = (out_round[:, None] == in_round[None, :]) & (group < GROUPS)[:, None]
    scale = 2.0 / math.sqrt(WINDOWS * COARSE * LANES)
    last = np.concatenate([np.cos(last), -np.sin(last)], axis=1) * scale
    last_hi, last_lo = split_bf16(np.where(np.tile(keep, 2), last, 0.0))
    return (
        *first,
        np.cos(twist).astype(np.float32),
        np.sin(twist).astype(np.float32),
        np.concatenate([last_hi, last_lo], axis=0),
    )


def whiten_kernel(spectra_hbm, *refs):
    inputs, (out_ref, *outputs), (spectra_ref, rows_ref, sems) = refs[:3], refs[3:7], refs[7:]
    pairs = [(spectra_hbm.at[0, n], spectra_ref.at[n]) for n in range(STATIONS_HERE)]
    pairs += zip(inputs, outputs)
    copies = [pltpu.make_async_copy(*pair, sems.at[n]) for n, pair in enumerate(pairs)]
    for copy in copies:
        copy.start()
    for station in range(STATIONS_HERE):
        copies[station].wait()
        for coarse in range(COARSE):
            rows_ref[pl.ds(coarse * 8 + station * 2, 2), :] = spectra_ref[
                station, :, pl.ds(coarse * LANES, LANES)
            ]
    even = lax.broadcasted_iota(jnp.int32, (8, LANES), 0) % 2 == 0
    power, total = [], None
    for coarse in range(COARSE):
        value = rows_ref[pl.ds(coarse * 8, 8), :]
        square = value * value
        other = jnp.where(even, pltpu.roll(square, 7, 0), pltpu.roll(square, 1, 0))
        power.append(square + other)
        total = power[-1] if total is None else total + power[-1]
    level = jnp.sum(total, axis=1, keepdims=True) * (1.0 / (COARSE * LANES))
    water = 0.05 * (level + 1e-06)
    white = [
        rows_ref[pl.ds(coarse * 8, 8), :] * lax.rsqrt(power[coarse] + water)
        for coarse in range(COARSE)
    ]
    turned = jnp.concatenate(white, axis=0).T.astype(jnp.bfloat16)
    for index in range(out_ref.shape[0]):
        out_ref[index] = turned
    for copy in copies[STATIONS_HERE:]:
        copy.wait()


def cross_kernel(mask_ref, all_ref, own_table, far_table, *refs):
    inputs, (out_ref, *outputs), (far_ref, left, right, sems) = refs[:3], refs[3:7], refs[7:]
    copies = [
        pltpu.make_async_copy(*pair, sems.at[n]) for n, pair in enumerate(zip(inputs, outputs))
    ]
    for copy in copies:
        copy.start()
    home = lax.axis_index("high")
    own = all_ref[pl.ds(pl.multiple_of(home * 128, 128), 128), :]
    left[...] = jnp.dot(own, own_table[...], preferred_element_type=jnp.float32)
    for r in range(ROUNDS):
        mask = mask_ref[r]
        high = (home ^ (mask >> 3)) & 7
        for block in range(8):
            start = pl.multiple_of(high * 128 + ((block ^ mask) & 7) * 16, 16)
            far_ref[pl.ds(r * 128 + block * 16, 16), :] = all_ref[pl.ds(start, 16), :]
    right[...] = jnp.dot(far_ref[...], far_table[...], preferred_element_type=jnp.float32)
    sublane = lax.broadcasted_iota(jnp.int32, (8, LANES), 0)
    odd_round = sublane // 2 % 2 == 1
    lower = lax.broadcasted_iota(jnp.int32, (8, LANES), 1) < PAIR_LANES

    for block in range(8):
        for i in range(STATIONS_HERE):
            straight = crossed = None
            sides = []
            for step in range(2):
                side = left[pl.ds(block * 16 + step * 8, 8), pl.ds(i * LANES, LANES)]
                sides.append((side, pltpu.roll(side, PAIR_LANES, 1)))
            for r in range(ROUNDS):
                total = None
                for step in range(2):
                    far_rows = pl.ds(r * 128 + block * 16 + step * 8, 8)
                    for part in range(2):
                        term = sides[step][part] * right[far_rows, pl.ds(part * LANES, LANES)]
                        total = term if total is None else total + term
                total = total + pltpu.roll(total, 4, 0)
                moved = pltpu.roll(total, 2, 0)
                straight = total if r == 0 else jnp.where(sublane >= 2 * r, total, straight)
                crossed = moved if r == 0 else jnp.where(sublane >= 2 * r, moved, crossed)
            first = jnp.where(odd_round, crossed, straight)
            second = jnp.where(odd_round, straight, crossed)
            slot = block * 8 + i * 2
            out_ref[slot] = jnp.where(
                lower, first, pltpu.roll(second, PAIR_LANES, 1)
            ).astype(jnp.bfloat16)
            out_ref[slot + 1] = jnp.where(
                lower, pltpu.roll(first, PAIR_LANES, 1), second
            ).astype(jnp.bfloat16)
    for copy in copies:
        copy.wait()


def split_value(value):
    high = value.astype(jnp.bfloat16)
    return high, (value - high.astype(jnp.float32)).astype(jnp.bfloat16)


def transform_kernel(spec_ref, first_ref, second_ref, cos_ref, sin_ref, last_ref, out_hbm, mid_ref, out_ref, sems):
    both = spec_ref[...].astype(jnp.float32).reshape(SHARES, 2, 8, LANES)
    spec = both[:, 0] + both[:, 1]
    share = lax.broadcasted_iota(jnp.int32, spec.shape, 0)
    row = lax.broadcasted_iota(jnp.int32, spec.shape, 1)
    lane = lax.broadcasted_iota(jnp.int32, spec.shape, 2)
    zero_bin = (share == 0) & (row % 2 == 0) & (lane < 4)
    spec = jnp.where(zero_bin, 0.5 * spec, spec).reshape(SHARES * 8, LANES)
    high, low = split_value(spec)
    half = SHARES * 4
    mid_ref[...] = jnp.dot(
        jnp.concatenate(
            [high[:half], low[:half], high[:half], high[half:], low[half:], high[half:]], axis=1
        ),
        jnp.concatenate([first_ref[...], second_ref[...]], axis=0),
        preferred_element_type=jnp.float32,
    )
    real, imag = [], []
    for pair in range(2):
        column_re, column_im = [], []
        for bit in range(2):
            y_re = mid_ref[:, pl.ds((bit * 4 + pair * 2) * LANES, LANES)]
            y_im = mid_ref[:, pl.ds((bit * 4 + pair * 2 + 1) * LANES, LANES)]
            c = cos_ref[:, pl.ds(bit * LANES, LANES)]
            s = sin_ref[:, pl.ds(bit * LANES, LANES)]
            column_re.append(y_re * c - y_im * s)
            column_im.append(y_re * s + y_im * c)
        real.append(jnp.concatenate(column_re, axis=0))
        imag.append(jnp.concatenate(column_im, axis=0))
    high, low = split_value(
        jnp.concatenate([jnp.concatenate(real, axis=1), jnp.concatenate(imag, axis=1)], axis=0)
    )
    double = jnp.dot(last_ref[...], high, preferred_element_type=jnp.float32)
    single = jnp.dot(
        last_ref[pl.ds(0, GROUP_ROWS), :], low, preferred_element_type=jnp.float32
    )
    total = double[:GROUP_ROWS] + double[GROUP_ROWS:] + single
    lags = out_ref.shape[2]
    copies = []
    for pair in range(2):
        for group in range(GROUPS):
            width = min(LANES, lags - group * LANES)
            out_ref[pair, :, pl.ds(group * LANES, width)] = total[
                group * ROUNDS : (group + 1) * ROUNDS, pair * LANES : pair * LANES + width
            ]
        copy = pltpu.make_async_copy(out_ref.at[pair], out_hbm.at[pair], sems.at[pair])
        copy.start()
        copies.append(copy)
    for copy in copies:
        copy.wait()


def spec_of(space):
    return pl.BlockSpec(memory_space=space)


def in_vmem(array):
    return pltpu.with_memory_space_constraint(jnp.asarray(array), VMEM)


def whiten(spectra, partner_masks, copies):
    tables = [jnp.asarray(table) for table in selection_tables()]
    return pl.pallas_call(
        whiten_kernel,
        out_shape=(
            pltpu.VMEM((copies, LANES, LANES), jnp.bfloat16),
            pltpu.SMEM((ROUNDS,), jnp.int32),
            *[pltpu.VMEM(table.shape, table.dtype) for table in tables],
        ),
        in_specs=[spec_of(pl.ANY)] * 4,
        out_specs=(spec_of(VMEM), spec_of(SMEM), *[spec_of(VMEM)] * 2),
        scratch_shapes=[
            pltpu.VMEM(spectra.shape[1:], jnp.float32),
            pltpu.VMEM((LANES, LANES), jnp.float32),
            pltpu.SemaphoreType.DMA((STATIONS_HERE + 3,)),
        ],
        name="whiten",
        interpret=INTERPRET,
    )(spectra, partner_masks, *tables)


def cross(partner_masks, gathered, own_table, far_table):
    tables = [jnp.asarray(table) for table in transform_tables()[2:]]
    return pl.pallas_call(
        cross_kernel,
        out_shape=(
            pltpu.VMEM((SLOTS, 8, LANES), jnp.bfloat16),
            *[pltpu.VMEM(table.shape, table.dtype) for table in tables],
        ),
        in_specs=[spec_of(SMEM)] + [spec_of(VMEM)] * 3 + [spec_of(pl.ANY)] * 3,
        out_specs=(spec_of(VMEM),) * 4,
        scratch_shapes=[
            pltpu.VMEM((512, LANES), jnp.bfloat16),
            pltpu.VMEM((LANES, 512), jnp.float32),
            pltpu.VMEM((512, 256), jnp.float32),
            pltpu.SemaphoreType.DMA((3,)),
        ],
        name="cross",
        interpret=INTERPRET,
    )(pltpu.with_memory_space_constraint(partner_masks, SMEM), *map(in_vmem, (gathered, own_table, far_table)), *tables)


def transform(spec_rows, *small_tables):
    return pl.pallas_call(
        transform_kernel,
        out_shape=jax.ShapeDtypeStruct((2, ROUNDS, 2 * MAXLAG), jnp.float32),
        in_specs=[spec_of(VMEM)] * 6,
        out_specs=spec_of(pl.ANY),
        scratch_shapes=[
            pltpu.VMEM((SHARES * 4, 1024), jnp.float32),
            pltpu.VMEM((2, ROUNDS, 2 * MAXLAG), jnp.float32),
            pltpu.SemaphoreType.DMA((2,)),
        ],
        name="transform",
        interpret=INTERPRET,
    )(*map(in_vmem, (spec_rows, *transform_tables()[:2], *small_tables)))


def body(spectra, partner_masks):
    rows, masks, own_table, far_table = whiten(
        spectra, partner_masks, lax.axis_size("high")
    )
    gathered = lax.all_to_all(
        rows.reshape(256, 4, LANES), ("high", "low", "near"), 0, 0, tiled=True
    )
    spec, *small_tables = cross(masks, gathered.reshape(1024, LANES), own_table, far_table)
    owned = lax.all_to_all(spec, ("low", "near", "core"), 0, 0, tiled=True)
    return transform(owned.reshape(SLOTS * 8, LANES), *small_tables)


def solution(mesh):
    devices = mesh.devices
    fine = Mesh(
        devices.reshape(8, devices.shape[0] // 8, devices.shape[1] // 2, 2),
        ("high", "low", "near", "core"),
    )
    return jax.shard_map(
        body,
        mesh=fine,
        in_specs=(P(("near", "core"), ("high", "low"), None, None), P()),
        out_specs=P(("high", "low", "near", "core"), None, None),
        check_vma=False,
    )
```

```python
import functools
import math

import jax
import jax.numpy as jnp
import numpy as np
from jax import lax
from jax.experimental import pallas as pl
from jax.experimental.pallas import tpu as pltpu
from jax.sharding import Mesh, PartitionSpec as P

NFFT = 8192
MAXLAG = 1200
LANES = 128
STATIONS_HERE = 4
ROUNDS = 4
WINDOWS = 8
COARSE = 16
SHARES = 32
SLOTS = 64
PAIR_LANES = 64
GROUPS = 19
GROUP_ROWS = 80
INTERPRET = False

VMEM = pltpu.MemorySpace.VMEM
SMEM = pltpu.MemorySpace.SMEM


def split_bf16(table):
    high = table.astype(jnp.bfloat16)
    low = (table - high.astype(np.float64)).astype(jnp.bfloat16)
    return high, low


@functools.lru_cache(None)
def selection_tables():
    lane = np.arange(LANES)
    coarse, station, part = lane // 8, lane // 2 % 4, lane % 2
    half, out_coarse, low, out_part = lane // 64, lane // 4 % 16, lane // 2 % 2, lane % 2
    same_bin = coarse[:, None] == out_coarse[None, :]
    own = [
        same_bin & (station == i)[:, None] & (part[:, None] == half[None, :])
        for i in range(STATIONS_HERE)
    ]
    far_station = same_bin & (station[:, None] == (2 * half + low)[None, :])
    match = np.where(out_part == 1, -1.0, 1.0) * (part[:, None] == out_part[None, :])
    cross = 1.0 * (part[:, None] != out_part[None, :])
    far = [far_station * np.where(half == side, match, cross) for side in range(2)]
    return (
        np.concatenate(own, axis=1).astype(jnp.bfloat16),
        np.concatenate(far, axis=1).astype(jnp.bfloat16),
    )


@functools.lru_cache(None)
def transform_tables():
    f = np.arange(LANES)
    shift = -MAXLAG % LANES
    base = (MAXLAG + shift) // LANES
    lane = np.arange(LANES)
    in_bit, coarse, pair, part = lane // 64, lane // 4 % 16, lane // 2 % 2, lane % 2
    first = []
    for side in range(2):
        steps = (2 * coarse + side)[:, None] * (f + shift)[None, :] % LANES
        cos, sin = np.cos(2 * np.pi * steps / LANES), np.sin(2 * np.pi * steps / LANES)
        real = np.where(part[:, None] == 0, cos, -sin)
        imag = np.where(part[:, None] == 0, sin, cos)
        table = np.concatenate(
            [
                np.where(((pair == p) & (in_bit == bit))[:, None], value, 0.0)
                for bit in range(2)
                for p in range(2)
                for value in (real, imag)
            ],
            axis=1,
        )
        high, low = split_bf16(table)
        first += [high, high, low]
    first = [np.concatenate(first[3 * side : 3 * side + 3], axis=0) for side in range(2)]
    row = np.arange(SHARES * 4)
    fine = 4 * (row // 8) + row % 2
    fine = np.repeat(np.stack([fine, fine + 2], axis=1), LANES, axis=1)
    twist = 2 * np.pi * (fine * np.tile(f + shift, 2)[None, :] % NFFT) / NFFT
    out_row = np.arange(GROUP_ROWS)
    group, out_round = out_row // ROUNDS, out_row % ROUNDS
    in_row = np.arange(SHARES * 8)
    in_fine = 4 * (in_row // 8 % 16) + 2 * (in_row // 128) + in_row % 2
    in_round = in_row // 2 % ROUNDS
    last = 2 * np.pi * (in_fine[None, :] * (group - base)[:, None] % 64) / 64
    keep = (out_round[:, None] == in_round[None, :]) & (group < GROUPS)[:, None]
    scale = 2.0 / math.sqrt(WINDOWS * COARSE * LANES)
    last = np.concatenate([np.cos(last), -np.sin(last)], axis=1) * scale
    last_hi, last_lo = split_bf16(np.where(np.tile(keep, 2), last, 0.0))
    return (
        *first,
        np.cos(twist).astype(np.float32),
        np.sin(twist).astype(np.float32),
        np.concatenate([last_hi, last_lo], axis=0),
    )


def whiten_kernel(spectra_hbm, *refs):
    inputs, (out_ref, *outputs), (spectra_ref, rows_ref, sems) = refs[:6], refs[6:13], refs[13:]
    pairs = [(spectra_hbm.at[0, n], spectra_ref.at[n]) for n in range(STATIONS_HERE)]
    pairs += zip(inputs, outputs)
    copies = [pltpu.make_async_copy(*pair, sems.at[n]) for n, pair in enumerate(pairs)]
    for n, copy in enumerate(copies):
        copy.start(priority=int(n >= STATIONS_HERE))
    for station in range(STATIONS_HERE):
        copies[station].wait()
        for coarse in range(COARSE):
            rows_ref[pl.ds(coarse * 8 + station * 2, 2), :] = spectra_ref[
                station, :, pl.ds(coarse * LANES, LANES)
            ]
    even = lax.broadcasted_iota(jnp.int32, (8, LANES), 0) % 2 == 0
    power, total = [], None
    for coarse in range(COARSE):
        value = rows_ref[pl.ds(coarse * 8, 8), :]
        square = value * value
        other = jnp.where(even, pltpu.roll(square, 7, 0), pltpu.roll(square, 1, 0))
        power.append(square + other)
        total = power[-1] if total is None else total + power[-1]
    level = jnp.sum(total, axis=1, keepdims=True) * (1.0 / (COARSE * LANES))
    water = 0.05 * (level + 1e-06)
    white = [
        rows_ref[pl.ds(coarse * 8, 8), :] * lax.rsqrt(power[coarse] + water)
        for coarse in range(COARSE)
    ]
    turned = jnp.concatenate(white, axis=0).T.astype(jnp.bfloat16)
    for index in range(out_ref.shape[0]):
        out_ref[index] = turned
    for copy in copies[STATIONS_HERE:]:
        copy.wait()


def cross_kernel(mask_ref, all_ref, own_table, far_table, out_ref, far_ref, left, right):
    home = lax.axis_index("high")
    own = all_ref[pl.ds(pl.multiple_of(home * 128, 128), 128), :]
    left[...] = jnp.dot(own, own_table[...], preferred_element_type=jnp.float32)
    for r in range(ROUNDS):
        mask = mask_ref[r]
        high = (home ^ (mask >> 3)) & 7
        for block in range(8):
            start = pl.multiple_of(high * 128 + ((block ^ mask) & 7) * 16, 16)
            far_ref[pl.ds(r * 128 + block * 16, 16), :] = all_ref[pl.ds(start, 16), :]
    right[...] = jnp.dot(far_ref[...], far_table[...], preferred_element_type=jnp.float32)
    sublane = lax.broadcasted_iota(jnp.int32, (8, LANES), 0)
    odd_round = sublane // 2 % 2 == 1
    lower = lax.broadcasted_iota(jnp.int32, (8, LANES), 1) < PAIR_LANES

    for block in range(8):
        for i in range(STATIONS_HERE):
            straight = crossed = None
            sides = []
            for step in range(2):
                side = left[pl.ds(block * 16 + step * 8, 8), pl.ds(i * LANES, LANES)]
                sides.append((side, pltpu.roll(side, PAIR_LANES, 1)))
            for r in range(ROUNDS):
                total = None
                for step in range(2):
                    far_rows = pl.ds(r * 128 + block * 16 + step * 8, 8)
                    for part in range(2):
                        term = sides[step][part] * right[far_rows, pl.ds(part * LANES, LANES)]
                        total = term if total is None else total + term
                total = total + pltpu.roll(total, 4, 0)
                moved = pltpu.roll(total, 2, 0)
                straight = total if r == 0 else jnp.where(sublane >= 2 * r, total, straight)
                crossed = moved if r == 0 else jnp.where(sublane >= 2 * r, moved, crossed)
            first = jnp.where(odd_round, crossed, straight)
            second = jnp.where(odd_round, straight, crossed)
            slot = block * 8 + i * 2
            out_ref[slot] = jnp.where(
                lower, first, pltpu.roll(second, PAIR_LANES, 1)
            ).astype(jnp.bfloat16)
            out_ref[slot + 1] = jnp.where(
                lower, pltpu.roll(first, PAIR_LANES, 1), second
            ).astype(jnp.bfloat16)


def split_value(value):
    high = value.astype(jnp.bfloat16)
    return high, (value - high.astype(jnp.float32)).astype(jnp.bfloat16)


def transform_kernel(spec_ref, first_ref, second_ref, cos_ref, sin_ref, last_ref, out_hbm, mid_ref, out_ref, sems):
    both = spec_ref[...].astype(jnp.float32).reshape(SHARES, 2, 8, LANES)
    spec = both[:, 0] + both[:, 1]
    share = lax.broadcasted_iota(jnp.int32, spec.shape, 0)
    row = lax.broadcasted_iota(jnp.int32, spec.shape, 1)
    lane = lax.broadcasted_iota(jnp.int32, spec.shape, 2)
    zero_bin = (share == 0) & (row % 2 == 0) & (lane < 4)
    spec = jnp.where(zero_bin, 0.5 * spec, spec).reshape(SHARES * 8, LANES)
    high, low = split_value(spec)
    half = SHARES * 4
    mid_ref[...] = jnp.dot(
        jnp.concatenate(
            [high[:half], low[:half], high[:half], high[half:], low[half:], high[half:]], axis=1
        ),
        jnp.concatenate([first_ref[...], second_ref[...]], axis=0),
        preferred_element_type=jnp.float32,
    )
    real, imag = [], []
    for pair in range(2):
        column_re, column_im = [], []
        for bit in range(2):
            y_re = mid_ref[:, pl.ds((bit * 4 + pair * 2) * LANES, LANES)]
            y_im = mid_ref[:, pl.ds((bit * 4 + pair * 2 + 1) * LANES, LANES)]
            c = cos_ref[:, pl.ds(bit * LANES, LANES)]
            s = sin_ref[:, pl.ds(bit * LANES, LANES)]
            column_re.append(y_re * c - y_im * s)
            column_im.append(y_re * s + y_im * c)
        real.append(jnp.concatenate(column_re, axis=0))
        imag.append(jnp.concatenate(column_im, axis=0))
    high, low = split_value(
        jnp.concatenate([jnp.concatenate(real, axis=1), jnp.concatenate(imag, axis=1)], axis=0)
    )
    double = jnp.dot(last_ref[...], high, preferred_element_type=jnp.float32)
    single = jnp.dot(
        last_ref[pl.ds(0, GROUP_ROWS), :], low, preferred_element_type=jnp.float32
    )
    total = double[:GROUP_ROWS] + double[GROUP_ROWS:] + single
    lags = out_ref.shape[2]
    copies = []
    for pair in range(2):
        for group in range(GROUPS):
            width = min(LANES, lags - group * LANES)
            out_ref[pair, :, pl.ds(group * LANES, width)] = total[
                group * ROUNDS : (group + 1) * ROUNDS, pair * LANES : pair * LANES + width
            ]
        copy = pltpu.make_async_copy(out_ref.at[pair], out_hbm.at[pair], sems.at[pair])
        copy.start()
        copies.append(copy)
    for copy in copies:
        copy.wait()


def spec_of(space):
    return pl.BlockSpec(memory_space=space)


def in_vmem(array):
    return pltpu.with_memory_space_constraint(jnp.asarray(array), VMEM)


def whiten(spectra, partner_masks, copies):
    tables = [jnp.asarray(table) for table in (*selection_tables(), *transform_tables()[2:])]
    return pl.pallas_call(
        whiten_kernel,
        out_shape=(
            pltpu.VMEM((copies, LANES, LANES), jnp.bfloat16),
            pltpu.SMEM((ROUNDS,), jnp.int32),
            *[pltpu.VMEM(table.shape, table.dtype) for table in tables],
        ),
        in_specs=[spec_of(pl.ANY)] * 7,
        out_specs=(spec_of(VMEM), spec_of(SMEM), *[spec_of(VMEM)] * 5),
        scratch_shapes=[
            pltpu.VMEM(spectra.shape[1:], jnp.float32),
            pltpu.VMEM((LANES, LANES), jnp.float32),
            pltpu.SemaphoreType.DMA((STATIONS_HERE + 6,)),
        ],
        name="whiten",
        interpret=INTERPRET,
    )(spectra, partner_masks, *tables)


def cross(partner_masks, gathered, own_table, far_table):
    return pl.pallas_call(
        cross_kernel,
        out_shape=pltpu.VMEM((SLOTS, 8, LANES), jnp.bfloat16),
        in_specs=[spec_of(SMEM)] + [spec_of(VMEM)] * 3,
        out_specs=spec_of(VMEM),
        scratch_shapes=[
            pltpu.VMEM((512, LANES), jnp.bfloat16),
            pltpu.VMEM((LANES, 512), jnp.float32),
            pltpu.VMEM((512, 256), jnp.float32),
        ],
        name="cross",
        interpret=INTERPRET,
    )(pltpu.with_memory_space_constraint(partner_masks, SMEM), *map(in_vmem, (gathered, own_table, far_table)))


def transform(spec_rows, *small_tables):
    return pl.pallas_call(
        transform_kernel,
        out_shape=jax.ShapeDtypeStruct((2, ROUNDS, 2 * MAXLAG), jnp.float32),
        in_specs=[spec_of(VMEM)] * 6,
        out_specs=spec_of(pl.ANY),
        scratch_shapes=[
            pltpu.VMEM((SHARES * 4, 1024), jnp.float32),
            pltpu.VMEM((2, ROUNDS, 2 * MAXLAG), jnp.float32),
            pltpu.SemaphoreType.DMA((2,)),
        ],
        name="transform",
        interpret=INTERPRET,
    )(*map(in_vmem, (spec_rows, *transform_tables()[:2], *small_tables)))


def body(spectra, partner_masks):
    rows, masks, own_table, far_table, *small_tables = whiten(
        spectra, partner_masks, lax.axis_size("high")
    )
    gathered = lax.all_to_all(
        rows.reshape(256, 4, LANES), ("high", "low", "near"), 0, 0, tiled=True
    )
    spec = cross(masks, gathered.reshape(1024, LANES), own_table, far_table)
    owned = lax.all_to_all(spec, ("low", "near", "core"), 0, 0, tiled=True)
    return transform(owned.reshape(SLOTS * 8, LANES), *small_tables)


def solution(mesh):
    devices = mesh.devices
    fine = Mesh(
        devices.reshape(8, devices.shape[0] // 8, devices.shape[1] // 2, 2),
        ("high", "low", "near", "core"),
    )
    return jax.shard_map(
        body,
        mesh=fine,
        in_specs=(P(("near", "core"), ("high", "low"), None, None), P()),
        out_specs=P(("high", "low", "near", "core"), None, None),
        check_vma=False,
    )
```
